1024 devices in a mesh: dom: 512 (over x, z, y), orb: 2 (over core).
Axes of the slice: x: 8, y: 8, z: 8, core: 2. Of those that a mesh axis runs over, the one named last changes fastest.
Arguments:
- block: float32 [256, 346112], P('orb', 'dom')
- conn: int32 [125, 4608], P(None, 'dom'), may hold values from 0 to 844, as said below
- bottom: int32 [86528], P('dom'), may hold values from 0 to 675, as said below
- cell_scale: float32 [4608], P('dom'), may hold values from 0.5 to 2
- potential: float32 [216, 4608], P(None, 'dom'), may hold values from 0.1 to 1
- mass: float32 [346112], P('dom'), may hold values from 0.5 to 2
- stiffness: float32 [125, 125], replicated, as said below
- interp: float32 [216, 125], replicated, may hold values from -0.5 to 0.5
- occupancy: float32 [256], P('orb'), may hold values from 0.2 to 2
- spectrum: float32 [2], replicated, as said below
Outputs:
- density: float32 [216, 4608], P(None, 'dom')
The draws below stay inside these ranges and needn't reach their ends.
Inputs may be any that keep to these rules, and one draw needn't show every extreme that they name: `conn`: for the cells of domain d an entry below 676 is one of d's own local node numbers and 676 + f names entry f of the next domain's list in bottom; every own node is named by some cell of its domain, and the cells form a conforming mesh. `bottom`: each domain's 169 entries are distinct local numbers of its own nodes. `stiffness`: symmetric and positive definite. spectrum[0] < spectrum[1].
All inputs are finite; a program needn't handle non-finite values.
Results may differ from the reference program's by a relative error of at most 0.0001.
Values sent between devices are 32-bit elements; how exact they have to be, the bound alone decides.
No kernel may reach another device: no remote copies, remote signals or barrier semaphores. Data moves between devices by JAX's collectives and lax.ppermute only.
A program may use at most 32 MiB of HBM per device.

```python
import math
import jax
import jax.numpy as jnp
from jax import lax

ORBS = 256
GRID = 3
LAYERS = 1
DEG = 3
NPC = 125
GAUSS = 216
FACE = 169
NODE_DEV = 676
CELL_DEV = 9
CELLS = 4608
NODES = 346112


def relabel_nodes(lone_element):
    rest = 1 + jax.random.permutation(lone_element, NODE_DEV - 2).astype(jnp.int32)
    ends = jnp.array([NODE_DEV - 1, 0], dtype=jnp.int32)
    return jnp.concatenate([ends, rest])


def mesh_tables(key):
    ndom = CELLS // CELL_DEV
    side = 4 * GRID + 1
    random_keys = jax.random.split(jax.random.fold_in(key, 17), ndom)
    sort_orders = jax.vmap(relabel_nodes)(random_keys).astype(jnp.int32)
    cell = jnp.arange(CELL_DEV, dtype=jnp.int32)
    corner_x = 4 * (cell % GRID)
    vertex_y_coord = 4 * (cell // GRID % GRID)
    vertex_z_coord = 4 * (cell // (GRID * GRID))
    local = jnp.arange(NPC, dtype=jnp.int32)
    node_x = corner_x[None, :] + local[:, None] % 5
    node_y = vertex_y_coord[None, :] + local[:, None] // 5 % 5
    node_z = vertex_z_coord[None, :] + local[:, None] // 25
    drawn = (node_z * side + node_y) * side + node_x
    ghost = NODE_DEV + node_y * side + node_x
    inside = node_z < 4 * LAYERS
    renamed = sort_orders[:, jnp.minimum(drawn, NODE_DEV - 1)]
    linked = jnp.where(inside[None], renamed, ghost[None])
    linked = jnp.transpose(linked, (1, 0, 2)).reshape(NPC, ndom * CELL_DEV)
    shared = sort_orders[:, jnp.arange(side * side, dtype=jnp.int32)].reshape(ndom * side * side)
    return (linked, shared)


def draw_conn(key, part):
    return mesh_tables(key)[0]


def draw_bottom(key, part):
    return mesh_tables(key)[1]


def draw_block(key, part):
    ndom = NODES // NODE_DEV
    first, second, third = jax.random.split(jax.random.fold_in(key, 3), 3)
    noise = jnp.clip(jax.random.normal(first, (ORBS, NODES), jnp.float32), -5.0, 5.0)
    common = jnp.clip(jax.random.normal(second, (NODES,), jnp.float32), -5.0, 5.0)
    loading = jax.random.uniform(third, (ORBS,), jnp.float32, 0.3, 1.0)
    domain = (jnp.arange(NODES, dtype=jnp.int32) // NODE_DEV).astype(jnp.float32)
    ramp = 1.0 + 2.0 * domain / max(ndom - 1, 1)
    return (noise + loading[:, None] * common[None, :]) * ramp[None, :]


def draw_stiffness(key, part):
    first, second = jax.random.split(jax.random.fold_in(key, 5), 2)
    raw = jax.random.uniform(first, (NPC, NPC), jnp.float32, -1.0, 1.0) * (1.5 / NPC)
    offdiag = (raw + raw.T) * 0.5 * (1.0 - jnp.eye(NPC, dtype=jnp.float32))
    diagonal = jax.random.uniform(second, (NPC,), jnp.float32, 1.5, 2.0)
    return offdiag + jnp.diag(diagonal)


def draw_spectrum(key, part):
    unit = jax.random.uniform(jax.random.fold_in(key, 7), (2,), jnp.float32, 0.0, 1.0)
    return jnp.stack([2.0 + 2.0 * unit[0], 40.0 + 20.0 * unit[1]])


def steps_of(rng, dims, shards, least, top_value):
    factor_of = 1.0
    for dim, blocks in shards:
        steps = jax.random.uniform(jax.random.fold_in(jax.random.fold_in(rng, 6), dim), (blocks,), jnp.float32, least / len(shards), top_value / len(shards))
        factor_of = factor_of * jnp.repeat(jnp.exp(steps), dims[dim] // blocks).reshape((-1,) + (1,) * (len(dims) - 1 - dim))
    return factor_of


def bell_draw(stream_key, dims, width, limit, kind=jnp.bfloat16):
    entries = width * jax.random.normal(stream_key, dims, jnp.float32)
    return jnp.clip(entries, min=-limit, max=limit).astype(kind)


def setup_inputs(seed: int = 0) -> dict:
    arg_keys = jax.random.split(jax.random.key(seed), 11)
    return {
        "block": draw_block(jax.random.fold_in(arg_keys[10], 71), 0),
        "conn": draw_conn(jax.random.fold_in(arg_keys[10], 71), 0),
        "bottom": draw_bottom(jax.random.fold_in(arg_keys[10], 71), 0),
        "cell_scale": jnp.clip(jnp.exp(math.log(2.0) - 1.3862944 * jax.random.uniform(arg_keys[3], (CELLS,), jnp.float32) ** steps_of(arg_keys[3], (CELLS,), ((0, 512),), -0.2, 0.2)), 0.5, 2.0),
        "potential": jnp.clip(jnp.exp(math.log(1.0) - 2.3025851 * jax.random.uniform(arg_keys[4], (GAUSS, CELLS), jnp.float32) ** steps_of(arg_keys[4], (GAUSS, CELLS), ((1, 512),), -0.2, 0.2)), 0.1, 1.0),
        "mass": jnp.clip(jnp.exp(math.log(2.0) - 1.3862944 * jax.random.uniform(arg_keys[5], (NODES,), jnp.float32) ** steps_of(arg_keys[5], (NODES,), ((0, 512),), -0.2, 0.2)), 0.5, 2.0),
        "stiffness": draw_stiffness(jax.random.fold_in(arg_keys[10], 71), 0),
        "interp": bell_draw(arg_keys[7], (GAUSS, NPC), NPC ** -0.5, 0.5, jnp.float32),
        "occupancy": jnp.clip(0.2 + 1.8 * jax.random.uniform(arg_keys[8], (ORBS,), jnp.float32) ** steps_of(arg_keys[8], (ORBS,), ((0, 2),), -0.2, 0.2), 0.2, 2.0),
        "spectrum": draw_spectrum(jax.random.fold_in(arg_keys[10], 71), 0),
    }


def cell_values(ext, conn):
    orbs = ext.shape[0]
    npc, cells = conn.shape
    picked = jnp.take(ext, conn.reshape(-1), axis=1).reshape(orbs, npc, cells)
    return jnp.transpose(picked, (1, 0, 2)).reshape(npc, orbs * cells)

def cell_apply(ext, conn, cell_scale, potential, stiffness, interp):
    orbs = ext.shape[0]
    npc, cells = conn.shape
    local = cell_values(ext, conn)
    stiff = jnp.dot(stiffness.astype(jnp.float32), local.astype(jnp.float32), precision=lax.Precision.HIGHEST, preferred_element_type=jnp.float32)
    quad = jnp.dot(interp.astype(jnp.float32), local.astype(jnp.float32), precision=lax.Precision.HIGHEST, preferred_element_type=jnp.float32)
    quad = quad.reshape(-1, orbs, cells) * potential[:, None, :]
    back = jnp.dot(interp.T.astype(jnp.float32), quad.reshape(-1, orbs * cells).astype(jnp.float32), precision=lax.Precision.HIGHEST, preferred_element_type=jnp.float32)
    total = stiff.reshape(npc, orbs, cells) * cell_scale[None, None, :] + back.reshape(npc, orbs, cells)
    values = jnp.transpose(total, (1, 0, 2)).reshape(orbs, npc * cells)
    return jnp.zeros_like(ext).at[:, conn.reshape(-1)].add(values)

def density_terms(ext, conn, interp, occupancy):
    orbs = ext.shape[0]
    npc, cells = conn.shape
    local = cell_values(ext, conn)
    quad = jnp.dot(interp.astype(jnp.float32), local.astype(jnp.float32), precision=lax.Precision.HIGHEST, preferred_element_type=jnp.float32)
    quad = quad.reshape(-1, orbs, cells)
    return jnp.sum(occupancy[None, :, None] * quad * quad, axis=1) / ORBS

def widen_matrix(field, bottom_d):
    faces = jax.vmap(lambda part, rows: part[:, rows])(field, bottom_d)
    ghost = jnp.concatenate([faces[1:], jnp.zeros_like(faces[:1])], axis=0)
    return jnp.concatenate([field, ghost], axis=2)

def apply_all(field, conn_d, scale_d, pot_d, bottom_d, mass_d, stiffness, interp):
    ext = widen_matrix(field, bottom_d)
    partial_value = lax.map(lambda items: cell_apply(items[0], items[1], items[2], items[3], stiffness, interp), (ext, conn_d, scale_d, pot_d))
    owned = partial_value[:, :, :NODE_DEV]
    rims = partial_value[:, :, NODE_DEV:]
    incoming = jnp.concatenate([jnp.zeros_like(rims[:1]), rims[:-1]], axis=0)
    owned = jax.vmap(lambda part, rows, extra: part.at[:, rows].add(extra))(owned, bottom_d, incoming)
    return owned / mass_d[:, None, :]

def reference(block, conn, bottom, cell_scale, potential, mass, stiffness, interp, occupancy, spectrum):
    ndom = cell_scale.shape[0] // CELL_DEV
    field = jnp.transpose(block.reshape(ORBS, ndom, NODE_DEV), (1, 0, 2))
    conn_d = jnp.transpose(conn.reshape(NPC, ndom, CELL_DEV), (1, 0, 2))
    pot_d = jnp.transpose(potential.reshape(GAUSS, ndom, CELL_DEV), (1, 0, 2))
    scale_d = cell_scale.reshape(ndom, CELL_DEV)
    bottom_d = bottom.reshape(ndom, FACE)
    mass_d = mass.reshape(ndom, NODE_DEV)
    halfwidth = (spectrum[1] - spectrum[0]) / 2.0
    centre = (spectrum[1] + spectrum[0]) / 2.0

    def operator(values):
        return apply_all(values, conn_d, scale_d, pot_d, bottom_d, mass_d, stiffness, interp)
    previous = field
    current = (operator(field) - centre * field) / halfwidth
    for step in range(DEG - 1):
        following = 2.0 * (operator(current) - centre * current) / halfwidth - previous
        previous = current
        current = following
    gram = jnp.einsum('dok,dpk->op', current * mass_d[:, None, :], current, precision=lax.Precision.HIGHEST) / (ndom * NODE_DEV)
    multiplier = jnp.linalg.cholesky(gram)
    inverse = jax.scipy.linalg.solve_triangular(multiplier, jnp.eye(ORBS, dtype=jnp.float32), lower=True)
    ortho = jnp.einsum('op,dpn->don', inverse, current, precision=lax.Precision.HIGHEST)
    ext = widen_matrix(ortho, bottom_d)
    dens = lax.map(lambda items: density_terms(items[0], items[1], interp, occupancy), (ext, conn_d))
    return jnp.transpose(dens, (1, 0, 2)).reshape(GAUSS, ndom * CELL_DEV)
```

```python
import functools

import jax
import jax.numpy as jnp
from jax import lax
from jax.experimental import pallas as pl
from jax.experimental.pallas import tpu as pltpu
from jax.sharding import Mesh
from jax.sharding import PartitionSpec as P

ORBS = 256
HALF = 128
DEG = 3
NPC = 125
GAUSS = 216
FACE = 169
OWN = 676
CELLS = 9
OWN_PAD = 680
FACE_PAD = 176
GHOST_AT = 768
EXT = 1024
PICK = CELLS * 128
ROWS = 1040
OCC_AT = OWN_PAD + FACE_PAD
FIELD = 864
VMEM = 24 * 1024 * 1024
F32 = jnp.float32
BF16 = jnp.bfloat16


def split(value):
    high = value.astype(BF16)
    return high, (value - high.astype(F32)).astype(BF16)


def dot(a, b, dims=((1,), (0,))):
    return lax.dot_general(a, b, (dims, ((), ())), preferred_element_type=F32)


def dot3(a, b, dims=((1,), (0,))):
    a_high, a_low = split(a)
    b_high, b_low = split(b)
    return dot(a_high, b_high, dims) + (dot(a_high, b_low, dims) + dot(a_low, b_high, dims))


def dot6(a, b, dims=((1,), (0,))):
    return lax.dot_general(
        a, b, (dims, ((), ())), precision=lax.Precision.HIGHEST, preferred_element_type=F32
    )


def put_split(ref, rows, value):
    high, low = split(value)
    ref[rows, 0:HALF] = high
    ref[rows, HALF : 2 * HALF] = low


def joined(value):
    return value[:, 0:HALF] + value[:, HALF : 2 * HALF]


def apply_cells(own, ghost, pick_ref, place_ref, matrix_ref, ext_ref, cell_ref, outs):
    ext_ref[OWN_PAD:GHOST_AT] = jnp.zeros((GHOST_AT - OWN_PAD, 2 * HALF), BF16)
    ext_ref[GHOST_AT + FACE_PAD : EXT] = jnp.zeros((EXT - GHOST_AT - FACE_PAD, 2 * HALF), BF16)
    put_split(ext_ref, slice(0, OWN_PAD), own)
    put_split(ext_ref, slice(GHOST_AT, GHOST_AT + FACE_PAD), ghost)
    picked = joined(dot(pick_ref[...], ext_ref[...]))
    for cell in range(CELLS):
        rows = slice(cell * 128, cell * 128 + 128)
        high, low = split(picked[rows])
        matrix_high, matrix_low = split(matrix_ref[rows])
        term = joined(dot(matrix_high, jnp.concatenate([high, low], axis=1)))
        put_split(cell_ref, rows, term + dot(matrix_low, high))
    total = joined(dot(place_ref[...], cell_ref[...]))
    own_out, ghost_out, bottom_out = outs
    own_out[...] = total[0:OWN_PAD]
    ghost_out[...] = total[OWN_PAD : OWN_PAD + FACE_PAD]
    bottom_out[...] = total[OWN_PAD + FACE_PAD : OWN_PAD + 2 * FACE_PAD]


def first_kernel(own, ghost, pick, place, matrix, own_out, ghost_out, bottom_out, ext, cell):
    outs = (own_out, ghost_out, bottom_out)
    apply_cells(own[...], ghost[...], pick, place, matrix, ext, cell, outs)


def next_values(step, refs):
    (beta, own_sum, ghost_sum, from_below, from_above, spread, own_scale, ghost_scale) = refs[:8]
    factor = 1.0 if step == 0 else 2.0
    high, low = split(from_below[...])
    arrived = dot(spread[...], high) + dot(spread[...], low)
    own = refs[8][...]
    ghost = refs[9][...]
    shift = beta[0]
    new_own = factor * (own_scale[...] * (own_sum[...] + arrived[0:OWN_PAD]) - shift * own)
    new_ghost = factor * (ghost_scale[...] * (ghost_sum[...] + from_above[...]) - shift * ghost)
    if step > 0:
        new_own = new_own - refs[10][...]
        new_ghost = new_ghost - refs[11][...]
    return new_own, new_ghost


def step_kernel(step, *refs):
    n = 10 if step == 0 else 12
    pick, place, matrix = refs[n : n + 3]
    new_own_out, new_ghost_out, own_out, ghost_out, bottom_out, ext, cell = refs[n + 3 :]
    own, ghost = next_values(step, refs)
    new_own_out[...] = own
    new_ghost_out[...] = ghost
    apply_cells(own, ghost, pick, place, matrix, ext, cell, (own_out, ghost_out, bottom_out))


def last_kernel(step, *refs):
    occ, out = refs[12:]
    own, ghost = next_values(step, refs)
    out[0:OWN_PAD] = own
    out[OWN_PAD:OCC_AT] = ghost
    out[OCC_AT:FIELD] = jnp.broadcast_to(occ[...], (FIELD - OCC_AT, HALF))


def eliminate(block):
    groups = HALF // 8
    rows = [block[8 * i : 8 * i + 8] for i in range(groups)]
    lane = lax.broadcasted_iota(jnp.int32, (1, HALF), 1)
    sub = lax.broadcasted_iota(jnp.int32, (8, 1), 0)
    for k in range(HALF):
        group, at = divmod(k, 8)
        row = rows[group][at : at + 1]
        pivot = jnp.where(lane == k, 1.0, row) * (1.0 / row[:, k : k + 1])
        for i in range(group, groups):
            new = jnp.where(lane == k, 0.0, rows[i]) - rows[i][:, k : k + 1] * pivot
            rows[i] = jnp.where(sub > at, new, rows[i]) if i == group else new
    done = jnp.concatenate(rows, axis=0)
    i = lax.broadcasted_iota(jnp.int32, (HALF, HALF), 0)
    j = lax.broadcasted_iota(jnp.int32, (HALF, HALF), 1)
    diagonal = jnp.sum(jnp.where(i == j, done, 0.0), axis=1, keepdims=True)
    lower = jnp.where(i > j, done, jnp.where(i == j, 1.0, 0.0))
    return lower * lax.rsqrt(diagonal)


def density_kernel(gram, field, pick, interp, out, inverse, work, ext, quad):
    work[...] = gram[0, 0:HALF]
    inverse[0:HALF, HALF:] = jnp.zeros((HALF, HALF), F32)

    def body(part, carry):
        block = eliminate(work[...])

        @pl.when(part == 0)
        def _():
            inverse[0:HALF, 0:HALF] = block
            side = dot6(gram[0, HALF:], block, ((1,), (1,)))
            inverse[HALF:, 0:HALF] = dot6(side, block)
            work[...] = gram[1, HALF:] - dot6(side, side, ((1,), (1,)))

        @pl.when(part == 1)
        def _():
            inverse[HALF:, HALF:] = block
            inverse[HALF:, 0:HALF] = -dot6(block, inverse[HALF:, 0:HALF])

        return carry

    ext[OWN_PAD:GHOST_AT] = jnp.zeros((GHOST_AT - OWN_PAD, 4 * HALF), BF16)
    ext[GHOST_AT + FACE_PAD : EXT] = jnp.zeros((EXT - GHOST_AT - FACE_PAD, 4 * HALF), BF16)
    for half in range(2):
        lanes = slice(half * HALF, half * HALF + HALF)
        low_lanes = slice(ORBS + half * HALF, ORBS + half * HALF + HALF)
        for rows, at in (
            (slice(0, OWN_PAD), slice(0, OWN_PAD)),
            (slice(GHOST_AT, GHOST_AT + FACE_PAD), slice(OWN_PAD, OCC_AT)),
        ):
            high, low = split(field[half, at])
            ext[rows, lanes] = high
            ext[rows, low_lanes] = low
    picked = dot(pick[...], ext[...])
    values = picked[:, 0:ORBS] + picked[:, ORBS:]
    for cell in range(CELLS):
        quad[cell] = dot3(interp[...], values[cell * 128 : cell * 128 + 128])
    lax.fori_loop(0, 2, body, 0)
    occ = jnp.concatenate([field[0, OCC_AT : OCC_AT + 1], field[1, OCC_AT : OCC_AT + 1]], axis=1)
    weights = occ * (1.0 / ORBS)
    inv_high, inv_low = split(inverse[...])
    for cell in range(CELLS):
        high, low = split(quad[cell])
        dims = ((1,), (1,))
        value = dot(high, inv_high, dims) + (dot(high, inv_low, dims) + dot(low, inv_high, dims))
        out[:, cell : cell + 1] = jnp.sum(value * value * weights, axis=1, keepdims=True)


def call(kernel, shapes, scratch, operands, scalars=0):
    out = [jax.ShapeDtypeStruct(shape, F32) for shape in shapes]
    in_vmem = pl.BlockSpec(memory_space=pltpu.VMEM)
    specs = [pl.BlockSpec(memory_space=pltpu.SMEM)] * scalars
    specs = specs + [in_vmem] * (len(operands) - scalars)
    return pl.pallas_call(
        kernel,
        out_shape=out,
        in_specs=specs,
        out_specs=[in_vmem] * len(out),
        scratch_shapes=scratch,
        compiler_params=pltpu.CompilerParams(vmem_limit_bytes=VMEM),
    )(*operands)


def gather_all(value, axes):
    count = lax.axis_size(axes)
    return lax.all_to_all(jnp.broadcast_to(value[None], (count,) + value.shape), axes, 0, 0)


def per_device(
    block, conn, bottom, cell_scale, potential, mass, stiffness, interp, occupancy, spectrum
):
    dom = ("x", "z", "y")
    count = lax.axis_size(dom)
    down = [(i + 1, i) for i in range(count - 1)]
    up = [(i, i + 1) for i in range(count - 1)]
    halfwidth = (spectrum[1] - spectrum[0]) / 2.0
    centre = (spectrum[1] + spectrum[0]) / 2.0

    own = jnp.pad(block.T, ((0, OWN_PAD - OWN), (0, 0)))
    masses = jnp.pad(jnp.take(mass, bottom), (0, 2 * HALF - FACE)).reshape(2, HALF)
    face = jnp.concatenate(
        [jnp.take(own, bottom, axis=0), masses, jnp.zeros((FACE_PAD - FACE - 2, HALF), F32)], axis=0
    )
    ghost = lax.ppermute(face, dom, down)
    ghost_mass = ghost[FACE : FACE + 2].reshape(-1)[:FACE_PAD]
    own_mass = jnp.pad(mass, (0, OWN_PAD - OWN))

    def inverse_mass(values, used):
        live = (jnp.arange(values.shape[0]) < used) & (values > 0.0)
        scale = jnp.where(live, 1.0 / (jnp.where(live, values, 1.0) * halfwidth), 0.0)
        return jnp.broadcast_to(scale[:, None], (values.shape[0], HALF))

    own_scale = inverse_mass(own_mass, OWN)
    ghost_scale = inverse_mass(ghost_mass, FACE)

    nodes = jnp.where(conn < OWN, conn, conn + (GHOST_AT - OWN))
    nodes = jnp.pad(nodes.T, ((0, 0), (0, 128 - NPC)), constant_values=-1).reshape(PICK)
    listed = jnp.pad(bottom, (0, FACE_PAD - FACE), constant_values=-2)
    targets = jnp.concatenate(
        [
            jnp.arange(OWN_PAD),
            GHOST_AT + jnp.arange(FACE_PAD),
            listed,
            jnp.full((ROWS - OWN_PAD - 2 * FACE_PAD,), -2),
        ]
    )
    pick = (nodes[:, None] == jnp.arange(EXT)[None, :]).astype(BF16)
    place = (targets[:, None] == nodes[None, :]).astype(BF16)
    spread = (jnp.arange(688)[:, None] == listed[None, :]).astype(BF16)

    wide = jnp.pad(interp, ((0, 0), (0, 128 - NPC)))
    weighted = (wide[:, None, :] * potential[:, :, None]).reshape(GAUSS, PICK)
    cells = dot6(weighted, wide, ((0,), (0,)))
    stiff = jnp.pad(stiffness, ((0, 128 - NPC), (0, 128 - NPC)))
    cells = cells + (cell_scale[:, None, None] * stiff[None]).reshape(PICK, 128)
    tables = (pick, place, cells)

    scratch = [pltpu.VMEM((EXT, 2 * HALF), BF16), pltpu.VMEM((PICK, 2 * HALF), BF16)]
    own_shape, face_shape = (OWN_PAD, HALF), (FACE_PAD, HALF)
    sums = call(
        first_kernel, [own_shape, face_shape, face_shape], scratch, (own, ghost) + tables
    )
    beta = (centre / halfwidth).reshape(1)
    last = ()
    for step in range(DEG):
        own_sum, ghost_sum, bottom_sum = sums
        from_above = lax.ppermute(bottom_sum, dom, down)
        from_below = lax.ppermute(ghost_sum, dom, up)
        operands = (beta, own_sum, ghost_sum, from_below, from_above, spread, own_scale)
        operands = operands + (ghost_scale, own, ghost) + last
        last = (own, ghost)
        if step < DEG - 1:
            own, ghost, *sums = call(
                functools.partial(step_kernel, step),
                [own_shape, face_shape, own_shape, face_shape, face_shape],
                scratch,
                operands + tables,
                1,
            )
    (field,) = call(
        functools.partial(last_kernel, DEG - 1),
        [(FIELD, HALF)],
        [],
        operands + (occupancy.reshape(1, HALF),),
        1,
    )
    whole = lax.all_gather(field, "orb", axis=0)

    weighted = field[:OWN_PAD] * own_mass[:, None]
    term = jnp.concatenate(
        [dot6(whole[half, :OWN_PAD], weighted, ((0,), (0,))) for half in range(2)], axis=0
    )
    planes = lax.axis_size("z") * lax.axis_size("y")
    term = term * (1.0 / (count * OWN))
    pieces = lax.all_to_all(term.reshape(planes, ORBS // planes, HALF), ("z", "y"), 0, 0)
    piece = jnp.sum(gather_all(jnp.sum(pieces, axis=0), "x"), axis=0)
    gram = gather_all(piece, ("orb", "z", "y")).reshape(2, ORBS, HALF)

    (density,) = call(
        density_kernel,
        [(GAUSS, CELLS)],
        [
            pltpu.VMEM((ORBS, ORBS), F32),
            pltpu.VMEM((HALF, HALF), F32),
            pltpu.VMEM((EXT, 4 * HALF), BF16),
            pltpu.VMEM((CELLS, GAUSS, ORBS), F32),
        ],
        (gram, whole, pick, wide),
    )
    return density


def solution(mesh):
    side = round(mesh.shape["dom"] ** (1.0 / 3.0))
    torus = Mesh(mesh.devices.reshape(side, side, side, 2), ("x", "z", "y", "orb"))
    dom = ("x", "z", "y")
    in_specs = (
        P("orb", dom),
        P(None, dom),
        P(dom),
        P(dom),
        P(None, dom),
        P(dom),
        P(),
        P(),
        P("orb"),
        P(),
    )
    return jax.shard_map(
        per_device, mesh=torus, in_specs=in_specs, out_specs=P(None, dom), check_vma=False
    )
```

```python
import functools

import jax
import jax.numpy as jnp
from jax import lax
from jax.experimental import pallas as pl
from jax.experimental.pallas import tpu as pltpu
from jax.sharding import Mesh
from jax.sharding import PartitionSpec as P

ORBS = 256
HALF = 128
DEG = 3
NPC = 125
GAUSS = 216
FACE = 169
OWN = 676
CELLS = 9
OWN_PAD = 680
FACE_PAD = 176
GHOST_AT = 768
EXT = 1024
PICK = CELLS * 128
ROWS = 1040
OCC_AT = OWN_PAD + FACE_PAD
FIELD = 864
VMEM = 24 * 1024 * 1024
F32 = jnp.float32
BF16 = jnp.bfloat16


def split(value):
    high = value.astype(BF16)
    return high, (value - high.astype(F32)).astype(BF16)


def dot(a, b, dims=((1,), (0,))):
    return lax.dot_general(a, b, (dims, ((), ())), preferred_element_type=F32)


def dot3(a, b, dims=((1,), (0,))):
    a_high, a_low = split(a)
    b_high, b_low = split(b)
    return dot(a_high, b_high, dims) + (dot(a_high, b_low, dims) + dot(a_low, b_high, dims))


def dot6(a, b, dims=((1,), (0,))):
    return lax.dot_general(
        a, b, (dims, ((), ())), precision=lax.Precision.HIGHEST, preferred_element_type=F32
    )


def put_split(ref, rows, value):
    high, low = split(value)
    ref[rows, 0:HALF] = high
    ref[rows, HALF : 2 * HALF] = low


def joined(value):
    return value[:, 0:HALF] + value[:, HALF : 2 * HALF]


def apply_cells(own, ghost, pick_ref, place_ref, matrix_ref, ext_ref, cell_ref, outs):
    ext_ref[OWN_PAD:GHOST_AT] = jnp.zeros((GHOST_AT - OWN_PAD, 2 * HALF), BF16)
    ext_ref[GHOST_AT + FACE_PAD : EXT] = jnp.zeros((EXT - GHOST_AT - FACE_PAD, 2 * HALF), BF16)
    put_split(ext_ref, slice(0, OWN_PAD), own)
    put_split(ext_ref, slice(GHOST_AT, GHOST_AT + FACE_PAD), ghost)
    picked = joined(dot(pick_ref[...], ext_ref[...]))
    for cell in range(CELLS):
        rows = slice(cell * 128, cell * 128 + 128)
        high, low = split(picked[rows])
        matrix_high, matrix_low = split(matrix_ref[rows])
        term = joined(dot(matrix_high, jnp.concatenate([high, low], axis=1)))
        put_split(cell_ref, rows, term + dot(matrix_low, high))
    total = joined(dot(place_ref[...], cell_ref[...]))
    own_out, ghost_out, bottom_out = outs
    own_out[...] = total[0:OWN_PAD]
    ghost_out[...] = total[OWN_PAD : OWN_PAD + FACE_PAD]
    bottom_out[...] = total[OWN_PAD + FACE_PAD : OWN_PAD + 2 * FACE_PAD]


def first_kernel(own, ghost, pick, place, matrix, own_out, ghost_out, bottom_out, ext, cell):
    outs = (own_out, ghost_out, bottom_out)
    apply_cells(own[...], ghost[...], pick, place, matrix, ext, cell, outs)


def next_values(step, refs):
    (beta, own_sum, ghost_sum, from_below, from_above, spread, own_scale, ghost_scale) = refs[:8]
    factor = 1.0 if step == 0 else 2.0
    high, low = split(from_below[...])
    arrived = dot(spread[...], high) + dot(spread[...], low)
    own = refs[8][...]
    ghost = refs[9][...]
    shift = beta[0]
    new_own = factor * (own_scale[...] * (own_sum[...] + arrived[0:OWN_PAD]) - shift * own)
    new_ghost = factor * (ghost_scale[...] * (ghost_sum[...] + from_above[...]) - shift * ghost)
    if step > 0:
        new_own = new_own - refs[10][...]
        new_ghost = new_ghost - refs[11][...]
    return new_own, new_ghost


def step_kernel(step, *refs):
    n = 10 if step == 0 else 12
    pick, place, matrix = refs[n : n + 3]
    new_own_out, new_ghost_out, own_out, ghost_out, bottom_out, ext, cell = refs[n + 3 :]
    own, ghost = next_values(step, refs)
    new_own_out[...] = own
    new_ghost_out[...] = ghost
    apply_cells(own, ghost, pick, place, matrix, ext, cell, (own_out, ghost_out, bottom_out))


def last_kernel(step, *refs):
    occ, out = refs[12:]
    own, ghost = next_values(step, refs)
    out[0:OWN_PAD] = own
    out[OWN_PAD:OCC_AT] = ghost
    out[OCC_AT:FIELD] = jnp.broadcast_to(occ[...], (FIELD - OCC_AT, HALF))


def reciprocal(value):
    guess = pl.reciprocal(value, approx=True)
    guess = guess * (2.0 - value * guess)
    return guess * (2.0 - value * guess)


def eliminate(block):
    groups = HALF // 8
    rows = [block[8 * i : 8 * i + 8] for i in range(groups)]
    lane = lax.broadcasted_iota(jnp.int32, (1, HALF), 1)
    sub = lax.broadcasted_iota(jnp.int32, (8, 1), 0)
    for k in range(0, HALF, 2):
        group, at = divmod(k, 8)
        left = [jnp.broadcast_to(rows[i][:, k : k + 1], (8, HALF)) for i in range(group, groups)]
        right = [
            jnp.broadcast_to(rows[i][:, k + 1 : k + 2], (8, HALF)) for i in range(group, groups)
        ]
        a = left[0][at : at + 1]
        b = left[0][at + 1 : at + 2]
        d = right[0][at + 1 : at + 2]
        scale = reciprocal(a * d - b * b)
        here, beside = lane == k, lane == k + 1
        upper = jnp.where(here, 1.0, jnp.where(beside, 0.0, rows[group][at : at + 1]))
        under = jnp.where(here, 0.0, jnp.where(beside, 1.0, rows[group][at + 1 : at + 2]))
        first = (d * upper - b * under) * scale
        second = (a * under - b * upper) * scale
        for i in range(group, groups):
            new = jnp.where(here | beside, 0.0, rows[i])
            new = new - left[i - group] * first - right[i - group] * second
            rows[i] = jnp.where(sub > at + 1, new, rows[i]) if i == group else new
    done = jnp.concatenate(rows, axis=0)
    i = lax.broadcasted_iota(jnp.int32, (HALF, HALF), 0)
    j = lax.broadcasted_iota(jnp.int32, (HALF, HALF), 1)
    odd = lax.broadcasted_iota(jnp.int32, (HALF, 1), 0) % 2 == 1
    diagonal = jnp.sum(jnp.where(i == j, done, 0.0), axis=1, keepdims=True)
    below = jnp.sum(jnp.where(i == j + 1, done, 0.0), axis=1, keepdims=True)
    lower = jnp.where(i // 2 > j // 2, done, jnp.where(i == j, 1.0, 0.0))
    ratio = jnp.where(odd, below / pltpu.roll(diagonal, 1, 0), 0.0)
    lower = lower - ratio * pltpu.roll(lower, 1, 0)
    return lower * lax.rsqrt(diagonal - ratio * below)


def density_kernel(gram, field, pick, interp, out, inverse, work, ext, quad):
    work[...] = gram[0, 0:HALF]
    inverse[0:HALF, HALF:] = jnp.zeros((HALF, HALF), F32)

    def body(part, carry):
        block = eliminate(work[...])

        @pl.when(part == 0)
        def _():
            inverse[0:HALF, 0:HALF] = block
            side = dot6(gram[0, HALF:], block, ((1,), (1,)))
            inverse[HALF:, 0:HALF] = dot6(side, block)
            work[...] = gram[1, HALF:] - dot6(side, side, ((1,), (1,)))

        @pl.when(part == 1)
        def _():
            inverse[HALF:, HALF:] = block
            inverse[HALF:, 0:HALF] = -dot6(block, inverse[HALF:, 0:HALF])

        return carry

    ext[OWN_PAD:GHOST_AT] = jnp.zeros((GHOST_AT - OWN_PAD, 4 * HALF), BF16)
    ext[GHOST_AT + FACE_PAD : EXT] = jnp.zeros((EXT - GHOST_AT - FACE_PAD, 4 * HALF), BF16)
    for half in range(2):
        lanes = slice(half * HALF, half * HALF + HALF)
        low_lanes = slice(ORBS + half * HALF, ORBS + half * HALF + HALF)
        for rows, at in (
            (slice(0, OWN_PAD), slice(0, OWN_PAD)),
            (slice(GHOST_AT, GHOST_AT + FACE_PAD), slice(OWN_PAD, OCC_AT)),
        ):
            high, low = split(field[half, at])
            ext[rows, lanes] = high
            ext[rows, low_lanes] = low
    picked = dot(pick[...], ext[...])
    values = picked[:, 0:ORBS] + picked[:, ORBS:]
    for cell in range(CELLS):
        quad[cell] = dot3(interp[...], values[cell * 128 : cell * 128 + 128])
    lax.fori_loop(0, 2, body, 0)
    occ = jnp.concatenate([field[0, OCC_AT : OCC_AT + 1], field[1, OCC_AT : OCC_AT + 1]], axis=1)
    weights = occ * (1.0 / ORBS)
    inv_high, inv_low = split(inverse[...])
    for cell in range(CELLS):
        high, low = split(quad[cell])
        dims = ((1,), (1,))
        value = dot(high, inv_high, dims) + (dot(high, inv_low, dims) + dot(low, inv_high, dims))
        out[:, cell : cell + 1] = jnp.sum(value * value * weights, axis=1, keepdims=True)


def call(kernel, shapes, scratch, operands, scalars=0):
    out = [jax.ShapeDtypeStruct(shape, F32) for shape in shapes]
    in_vmem = pl.BlockSpec(memory_space=pltpu.VMEM)
    specs = [pl.BlockSpec(memory_space=pltpu.SMEM)] * scalars
    specs = specs + [in_vmem] * (len(operands) - scalars)
    return pl.pallas_call(
        kernel,
        out_shape=out,
        in_specs=specs,
        out_specs=[in_vmem] * len(out),
        scratch_shapes=scratch,
        compiler_params=pltpu.CompilerParams(vmem_limit_bytes=VMEM),
    )(*operands)


def gather_all(value, axes):
    count = lax.axis_size(axes)
    return lax.all_to_all(jnp.broadcast_to(value[None], (count,) + value.shape), axes, 0, 0)


def per_device(
    block, conn, bottom, cell_scale, potential, mass, stiffness, interp, occupancy, spectrum
):
    dom = ("x", "zh", "zl", "y")
    count = lax.axis_size(dom)
    down = [(i + 1, i) for i in range(count - 1)]
    up = [(i, i + 1) for i in range(count - 1)]
    halfwidth = (spectrum[1] - spectrum[0]) / 2.0
    centre = (spectrum[1] + spectrum[0]) / 2.0

    own = jnp.pad(block.T, ((0, OWN_PAD - OWN), (0, 0)))
    masses = jnp.pad(jnp.take(mass, bottom), (0, 2 * HALF - FACE)).reshape(2, HALF)
    face = jnp.concatenate(
        [jnp.take(own, bottom, axis=0), masses, jnp.zeros((FACE_PAD - FACE - 2, HALF), F32)], axis=0
    )
    ghost = lax.ppermute(face, dom, down)
    ghost_mass = ghost[FACE : FACE + 2].reshape(-1)[:FACE_PAD]
    own_mass = jnp.pad(mass, (0, OWN_PAD - OWN))

    def inverse_mass(values, used):
        live = (jnp.arange(values.shape[0]) < used) & (values > 0.0)
        scale = jnp.where(live, 1.0 / (jnp.where(live, values, 1.0) * halfwidth), 0.0)
        return jnp.broadcast_to(scale[:, None], (values.shape[0], HALF))

    own_scale = inverse_mass(own_mass, OWN)
    ghost_scale = inverse_mass(ghost_mass, FACE)

    nodes = jnp.where(conn < OWN, conn, conn + (GHOST_AT - OWN))
    nodes = jnp.pad(nodes.T, ((0, 0), (0, 128 - NPC)), constant_values=-1).reshape(PICK)
    listed = jnp.pad(bottom, (0, FACE_PAD - FACE), constant_values=-2)
    targets = jnp.concatenate(
        [
            jnp.arange(OWN_PAD),
            GHOST_AT + jnp.arange(FACE_PAD),
            listed,
            jnp.full((ROWS - OWN_PAD - 2 * FACE_PAD,), -2),
        ]
    )
    pick = (nodes[:, None] == jnp.arange(EXT)[None, :]).astype(BF16)
    place = (targets[:, None] == nodes[None, :]).astype(BF16)
    spread = (jnp.arange(688)[:, None] == listed[None, :]).astype(BF16)

    wide = jnp.pad(interp, ((0, 0), (0, 128 - NPC)))
    weighted = (wide[:, None, :] * potential[:, :, None]).reshape(GAUSS, PICK)
    cells = dot6(weighted, wide, ((0,), (0,)))
    stiff = jnp.pad(stiffness, ((0, 128 - NPC), (0, 128 - NPC)))
    cells = cells + (cell_scale[:, None, None] * stiff[None]).reshape(PICK, 128)
    tables = (pick, place, cells)

    scratch = [pltpu.VMEM((EXT, 2 * HALF), BF16), pltpu.VMEM((PICK, 2 * HALF), BF16)]
    own_shape, face_shape = (OWN_PAD, HALF), (FACE_PAD, HALF)
    sums = call(
        first_kernel, [own_shape, face_shape, face_shape], scratch, (own, ghost) + tables
    )
    beta = (centre / halfwidth).reshape(1)
    last = ()
    for step in range(DEG):
        own_sum, ghost_sum, bottom_sum = sums
        from_above = lax.ppermute(bottom_sum, dom, down)
        from_below = lax.ppermute(ghost_sum, dom, up)
        operands = (beta, own_sum, ghost_sum, from_below, from_above, spread, own_scale)
        operands = operands + (ghost_scale, own, ghost) + last
        last = (own, ghost)
        if step < DEG - 1:
            own, ghost, *sums = call(
                functools.partial(step_kernel, step),
                [own_shape, face_shape, own_shape, face_shape, face_shape],
                scratch,
                operands + tables,
                1,
            )
    (field,) = call(
        functools.partial(last_kernel, DEG - 1),
        [(FIELD, HALF)],
        [],
        operands + (occupancy.reshape(1, HALF),),
        1,
    )
    whole = lax.all_gather(field, "orb", axis=0)

    weighted = field[:OWN_PAD] * own_mass[:, None]
    term = jnp.concatenate(
        [dot6(whole[half, :OWN_PAD], weighted, ((0,), (0,))) for half in range(2)], axis=0
    )
    near, far = ("zl", "y"), ("x", "zh")
    size = lax.axis_size(near)
    term = term * (1.0 / (count * OWN))
    pieces = lax.all_to_all(term.reshape(size, ORBS // size, HALF), near, 0, 0)
    piece = jnp.sum(gather_all(jnp.sum(pieces, axis=0), far), axis=0)
    gram = lax.all_gather(gather_all(piece, near).reshape(ORBS, HALF), "orb", axis=0)

    (density,) = call(
        density_kernel,
        [(GAUSS, CELLS)],
        [
            pltpu.VMEM((ORBS, ORBS), F32),
            pltpu.VMEM((HALF, HALF), F32),
            pltpu.VMEM((EXT, 4 * HALF), BF16),
            pltpu.VMEM((CELLS, GAUSS, ORBS), F32),
        ],
        (gram, whole, pick, wide),
    )
    return density


def solution(mesh):
    side = round(mesh.shape["dom"] ** (1.0 / 3.0))
    shape = (side, side // 2, 2, side, 2)
    torus = Mesh(mesh.devices.reshape(shape), ("x", "zh", "zl", "y", "orb"))
    dom = ("x", "zh", "zl", "y")
    in_specs = (
        P("orb", dom),
        P(None, dom),
        P(dom),
        P(dom),
        P(None, dom),
        P(dom),
        P(),
        P(),
        P("orb"),
        P(),
    )
    return jax.shard_map(
        per_device, mesh=torus, in_specs=in_specs, out_specs=P(None, dom), check_vma=False
    )
```

```python
import functools

import jax
import jax.numpy as jnp
from jax import lax
from jax.experimental import pallas as pl
from jax.experimental.pallas import tpu as pltpu
from jax.sharding import Mesh
from jax.sharding import PartitionSpec as P

ORBS = 256
HALF = 128
DEG = 3
NPC = 125
GAUSS = 216
FACE = 169
OWN = 676
CELLS = 9
OWN_PAD = 680
FACE_PAD = 176
GHOST_AT = 768
EXT = 1024
PICK = CELLS * 128
ROWS = 1040
OCC_AT = OWN_PAD + FACE_PAD
FIELD = 864
DOM = ("xh", "xl", "zh", "zm", "zl", "yh", "yl")
VMEM = 24 * 1024 * 1024
F32 = jnp.float32
BF16 = jnp.bfloat16


def split(value):
    high = value.astype(BF16)
    return high, (value - high.astype(F32)).astype(BF16)


def dot(a, b, dims=((1,), (0,))):
    return lax.dot_general(a, b, (dims, ((), ())), preferred_element_type=F32)


def dot3(a, b, dims=((1,), (0,))):
    a_high, a_low = split(a)
    b_high, b_low = split(b)
    return dot(a_high, b_high, dims) + (dot(a_high, b_low, dims) + dot(a_low, b_high, dims))


def dot6(a, b, dims=((1,), (0,))):
    return lax.dot_general(
        a, b, (dims, ((), ())), precision=lax.Precision.HIGHEST, preferred_element_type=F32
    )


def put_split(ref, rows, value):
    high, low = split(value)
    ref[rows, 0:HALF] = high
    ref[rows, HALF : 2 * HALF] = low


def joined(value):
    return value[:, 0:HALF] + value[:, HALF : 2 * HALF]


def apply_cells(own, ghost, pick_ref, place_ref, matrix_ref, ext_ref, cell_ref, outs):
    ext_ref[OWN_PAD:GHOST_AT] = jnp.zeros((GHOST_AT - OWN_PAD, 2 * HALF), BF16)
    ext_ref[GHOST_AT + FACE_PAD : EXT] = jnp.zeros((EXT - GHOST_AT - FACE_PAD, 2 * HALF), BF16)
    put_split(ext_ref, slice(0, OWN_PAD), own)
    put_split(ext_ref, slice(GHOST_AT, GHOST_AT + FACE_PAD), ghost)
    picked = joined(dot(pick_ref[...], ext_ref[...]))
    for cell in range(CELLS):
        rows = slice(cell * 128, cell * 128 + 128)
        high, low = split(picked[rows])
        matrix_high, matrix_low = split(matrix_ref[rows])
        term = joined(dot(matrix_high, jnp.concatenate([high, low], axis=1)))
        put_split(cell_ref, rows, term + dot(matrix_low, high))
    total = joined(dot(place_ref[...], cell_ref[...]))
    own_out, ghost_out, bottom_out = outs
    own_out[...] = total[0:OWN_PAD]
    ghost_out[...] = total[OWN_PAD : OWN_PAD + FACE_PAD]
    bottom_out[...] = total[OWN_PAD + FACE_PAD : OWN_PAD + 2 * FACE_PAD]


def column(row):
    return jnp.broadcast_to(row, (HALF, HALF)).T


def one_hot(left, right):
    return jnp.where(left == right, 1.0, 0.0).astype(BF16)


def face_kernel(block, bottom, mass, face, own, spread, listed, terms, select, ext):
    own[0:OWN] = block[...]
    own[OWN:OWN_PAD] = jnp.zeros((OWN_PAD - OWN, HALF), F32)
    ext[OWN_PAD:GHOST_AT] = jnp.zeros((GHOST_AT - OWN_PAD, 2 * HALF), BF16)
    put_split(ext, slice(0, OWN_PAD), own[...])
    listed[...] = jnp.full(listed.shape, -2.0, F32)
    listed[0:1, 0:FACE] = bottom[...].astype(F32)
    lane = lax.broadcasted_iota(jnp.int32, (1, HALF), 1).astype(F32)
    for at in range(0, FACE_PAD, HALF):
        size = min(HALF, FACE_PAD - at)
        wanted = column(listed[0:1, at : at + HALF])[0:size]
        for start in range(0, GHOST_AT, HALF):
            select[at : at + size, start : start + HALF] = one_hot(wanted, lane + float(start))
    node = lax.broadcasted_iota(jnp.int32, (GHOST_AT, 2 * HALF), 0).astype(F32)
    spread[...] = one_hot(node, listed[0:1])
    terms[...] = jnp.zeros(terms.shape, F32)
    terms[0:1, 0:OWN] = mass[...]
    rest = terms[0:1]
    for term in range(3):
        part = rest.astype(BF16).astype(F32)
        terms[term : term + 1] = part
        rest = rest - part
    parts = dot(terms[...].astype(BF16), spread[...])
    masses = parts[0:1] + (parts[1:2] + parts[2:3])
    face[...] = joined(dot(select[...], ext[...]))
    face[FACE : FACE + 1] = masses[:, 0:HALF]
    face[FACE + 1 : FACE + 2] = masses[:, HALF:]


def halfwidth_of(spectrum):
    low = jnp.full((1, HALF), spectrum[0], F32)
    high = jnp.full((1, HALF), spectrum[1], F32)
    return (high - low) * 0.5, (high + low) * 0.5


def table_kernel(
    spectrum,
    scales,
    conn,
    bottom,
    interp,
    potential,
    stiffness,
    mass,
    pick,
    place,
    matrix,
    own_scale,
    wide,
    nodes,
    listed,
    targets,
    square,
    points,
    weight,
    masses,
):
    nodes[...] = jnp.full(nodes.shape, -1.0, F32)
    own_node = conn[...] < OWN
    named = jnp.where(own_node, conn[...], conn[...] + (GHOST_AT - OWN))
    nodes[0:CELLS, 0:NPC] = named.astype(F32)
    listed[...] = jnp.full(listed.shape, -2.0, F32)
    listed[0:1, 0:FACE] = bottom[...].astype(F32)
    lane = lax.broadcasted_iota(jnp.int32, (1, HALF), 1).astype(F32)
    targets[...] = jnp.full(targets.shape, -2.0, F32)
    row = lax.broadcasted_iota(jnp.int32, (OWN_PAD, HALF), 0).astype(F32)
    targets[0:OWN_PAD] = row
    targets[OWN_PAD:OCC_AT] = row[0:FACE_PAD] + float(GHOST_AT)
    for at in range(0, FACE_PAD, HALF):
        size = min(HALF, FACE_PAD - at)
        targets[OCC_AT + at : OCC_AT + at + size] = column(listed[0:1, at : at + HALF])[0:size]
    square[...] = jnp.zeros(square.shape, F32)
    square[0:NPC, 0:NPC] = stiffness[...]
    points[...] = jnp.zeros(points.shape, F32)
    points[0:GAUSS, 0:NPC] = interp[...]
    wide[...] = points[0:GAUSS]
    weight[...] = jnp.zeros(weight.shape, F32)
    weight[0:CELLS, 0:GAUSS] = potential[...]
    flipped = jnp.concatenate([points[0:HALF].T, points[HALF:].T], axis=1)
    high, low = split(points[...])
    both = jnp.concatenate([high, low], axis=1)
    for cell in range(CELLS):
        rows = slice(cell * HALF, cell * HALF + HALF)
        named = nodes[cell : cell + 1]
        wanted = column(named)
        for start in range(0, EXT, HALF):
            pick[rows, start : start + HALF] = one_hot(wanted, lane + float(start))
        place[:, rows] = one_hot(targets[...], named)
        left_high, left_low = split(flipped * weight[cell : cell + 1])
        product = joined(dot(left_high, both)) + dot(left_low, high)
        matrix[rows] = product + scales[cell] * square[...]
    masses[...] = jnp.ones(masses.shape, F32)
    masses[0:1, 0:OWN] = mass[...]
    halfwidth, _ = halfwidth_of(spectrum)
    for at in range(0, OWN_PAD, HALF):
        size = min(HALF, OWN_PAD - at)
        own_scale[at : at + size] = 1.0 / (column(masses[0:1, at : at + HALF])[0:size] * halfwidth)


def first_kernel(
    spectrum, own, ghost, pick, place, matrix, own_out, ghost_out, bottom_out, scale_out, ext, cell
):
    outs = (own_out, ghost_out, bottom_out)
    apply_cells(own[...], ghost[...], pick, place, matrix, ext, cell, outs)
    halfwidth, _ = halfwidth_of(spectrum)
    node = lax.broadcasted_iota(jnp.int32, (FACE_PAD, HALF), 0)
    for at in range(0, FACE_PAD, HALF):
        size = min(HALF, FACE_PAD - at)
        mass_row = FACE + at // HALF
        mass = column(ghost[mass_row : mass_row + 1])[0:size]
        live = (mass > 0.0) & (node[at : at + size] < FACE)
        scale = 1.0 / (jnp.where(live, mass, 1.0) * halfwidth)
        scale_out[at : at + size] = jnp.where(live, scale, 0.0)


def next_values(step, refs):
    (spectrum, own_sum, ghost_sum, from_below, from_above, spread, own_scale, ghost_scale) = refs[:8]
    factor = 1.0 if step == 0 else 2.0
    high, low = split(from_below[...])
    arriving = jnp.concatenate([high, low], axis=1)
    arriving = jnp.concatenate([arriving, jnp.zeros((2 * HALF - FACE_PAD, 2 * HALF), BF16)], axis=0)
    arrived = joined(dot(spread[...], arriving))
    own = refs[8][...]
    ghost = refs[9][...]
    halfwidth, centre = halfwidth_of(spectrum)
    shift = centre / halfwidth
    new_own = factor * (own_scale[...] * (own_sum[...] + arrived[0:OWN_PAD]) - shift * own)
    new_ghost = factor * (ghost_scale[...] * (ghost_sum[...] + from_above[...]) - shift * ghost)
    if step > 0:
        new_own = new_own - refs[10][...]
        new_ghost = new_ghost - refs[11][...]
    return new_own, new_ghost


def step_kernel(step, *refs):
    n = 10 if step == 0 else 12
    pick, place, matrix = refs[n : n + 3]
    new_own_out, new_ghost_out, own_out, ghost_out, bottom_out, ext, cell = refs[n + 3 :]
    own, ghost = next_values(step, refs)
    new_own_out[...] = own
    new_ghost_out[...] = ghost
    apply_cells(own, ghost, pick, place, matrix, ext, cell, (own_out, ghost_out, bottom_out))


def last_kernel(step, *refs):
    occ, out = refs[12:]
    own, ghost = next_values(step, refs)
    out[0:OWN_PAD] = own
    out[OWN_PAD:OCC_AT] = ghost
    out[OCC_AT:FIELD] = jnp.broadcast_to(occ[...], (FIELD - OCC_AT, HALF))


def reciprocal(value):
    guess = pl.reciprocal(value, approx=True)
    guess = guess * (2.0 - value * guess)
    return guess * (2.0 - value * guess)


def eliminate(block):
    groups = HALF // 8
    rows = [block[8 * i : 8 * i + 8] for i in range(groups)]
    lane = lax.broadcasted_iota(jnp.int32, (1, HALF), 1)
    sub = lax.broadcasted_iota(jnp.int32, (8, 1), 0)
    for k in range(0, HALF, 2):
        group, at = divmod(k, 8)
        left = [jnp.broadcast_to(rows[i][:, k : k + 1], (8, HALF)) for i in range(group, groups)]
        right = [
            jnp.broadcast_to(rows[i][:, k + 1 : k + 2], (8, HALF)) for i in range(group, groups)
        ]
        a = left[0][at : at + 1]
        b = left[0][at + 1 : at + 2]
        d = right[0][at + 1 : at + 2]
        scale = reciprocal(a * d - b * b)
        here, beside = lane == k, lane == k + 1
        upper = jnp.where(here, 1.0, jnp.where(beside, 0.0, rows[group][at : at + 1]))
        under = jnp.where(here, 0.0, jnp.where(beside, 1.0, rows[group][at + 1 : at + 2]))
        first = (d * upper - b * under) * scale
        second = (a * under - b * upper) * scale
        for i in range(group, groups):
            new = jnp.where(here | beside, 0.0, rows[i])
            new = new - left[i - group] * first - right[i - group] * second
            rows[i] = jnp.where(sub > at + 1, new, rows[i]) if i == group else new
    done = jnp.concatenate(rows, axis=0)
    i = lax.broadcasted_iota(jnp.int32, (HALF, HALF), 0)
    j = lax.broadcasted_iota(jnp.int32, (HALF, HALF), 1)
    odd = lax.broadcasted_iota(jnp.int32, (HALF, 1), 0) % 2 == 1
    diagonal = jnp.sum(jnp.where(i == j, done, 0.0), axis=1, keepdims=True)
    below = jnp.sum(jnp.where(i == j + 1, done, 0.0), axis=1, keepdims=True)
    lower = jnp.where(i // 2 > j // 2, done, jnp.where(i == j, 1.0, 0.0))
    ratio = jnp.where(odd, below / pltpu.roll(diagonal, 1, 0), 0.0)
    lower = lower - ratio * pltpu.roll(lower, 1, 0)
    return lower * lax.rsqrt(diagonal - ratio * below)


def density_kernel(gram, field, pick, interp, out, inverse, work, ext, quad):
    work[...] = gram[0, 0:HALF]
    inverse[0:HALF, HALF:] = jnp.zeros((HALF, HALF), F32)

    def body(part, carry):
        block = eliminate(work[...])

        @pl.when(part == 0)
        def _():
            inverse[0:HALF, 0:HALF] = block
            side = dot6(gram[0, HALF:], block, ((1,), (1,)))
            inverse[HALF:, 0:HALF] = dot6(side, block)
            work[...] = gram[1, HALF:] - dot6(side, side, ((1,), (1,)))

        @pl.when(part == 1)
        def _():
            inverse[HALF:, HALF:] = block
            inverse[HALF:, 0:HALF] = -dot6(block, inverse[HALF:, 0:HALF])

        return carry

    ext[OWN_PAD:GHOST_AT] = jnp.zeros((GHOST_AT - OWN_PAD, 4 * HALF), BF16)
    ext[GHOST_AT + FACE_PAD : EXT] = jnp.zeros((EXT - GHOST_AT - FACE_PAD, 4 * HALF), BF16)
    for half in range(2):
        lanes = slice(half * HALF, half * HALF + HALF)
        low_lanes = slice(ORBS + half * HALF, ORBS + half * HALF + HALF)
        for rows, at in (
            (slice(0, OWN_PAD), slice(0, OWN_PAD)),
            (slice(GHOST_AT, GHOST_AT + FACE_PAD), slice(OWN_PAD, OCC_AT)),
        ):
            high, low = split(field[half, at])
            ext[rows, lanes] = high
            ext[rows, low_lanes] = low
    picked = dot(pick[...], ext[...])
    values = picked[:, 0:ORBS] + picked[:, ORBS:]
    for cell in range(CELLS):
        quad[cell] = dot3(interp[...], values[cell * 128 : cell * 128 + 128])
    lax.fori_loop(0, 2, body, 0)
    occ = jnp.concatenate([field[0, OCC_AT : OCC_AT + 1], field[1, OCC_AT : OCC_AT + 1]], axis=1)
    weights = occ * (1.0 / ORBS)
    inv_high, inv_low = split(inverse[...])
    for cell in range(CELLS):
        high, low = split(quad[cell])
        dims = ((1,), (1,))
        value = dot(high, inv_high, dims) + (dot(high, inv_low, dims) + dot(low, inv_high, dims))
        out[:, cell : cell + 1] = jnp.sum(value * value * weights, axis=1, keepdims=True)


def call(kernel, shapes, scratch, operands, scalars=0):
    out = [jax.ShapeDtypeStruct(shape[:2], (shape + (F32,))[2]) for shape in shapes]
    in_vmem = pl.BlockSpec(memory_space=pltpu.VMEM)
    specs = [pl.BlockSpec(memory_space=pltpu.SMEM)] * scalars
    specs = specs + [in_vmem] * (len(operands) - scalars)
    return pl.pallas_call(
        kernel,
        out_shape=out,
        in_specs=specs,
        out_specs=[in_vmem] * len(out),
        scratch_shapes=scratch,
        compiler_params=pltpu.CompilerParams(vmem_limit_bytes=VMEM),
    )(*operands)


def gather_all(value, axes):
    count = lax.axis_size(axes)
    return lax.all_to_all(jnp.broadcast_to(value[None], (count,) + value.shape), axes, 0, 0)


def per_device(
    block, conn, bottom, cell_scale, potential, mass, stiffness, interp, occupancy, spectrum
):
    dom = DOM
    count = lax.axis_size(dom)
    down = [(i + 1, i) for i in range(count - 1)]
    up = [(i, i + 1) for i in range(count - 1)]
    listed = bottom.reshape(1, FACE)
    mass_row = mass.reshape(1, OWN)
    face, own, spread = call(
        face_kernel,
        [(FACE_PAD, HALF), (OWN_PAD, HALF), (GHOST_AT, 2 * HALF, BF16)],
        [
            pltpu.VMEM((8, 2 * HALF), F32),
            pltpu.VMEM((8, GHOST_AT), F32),
            pltpu.VMEM((FACE_PAD, GHOST_AT), BF16),
            pltpu.VMEM((GHOST_AT, 2 * HALF), BF16),
        ],
        (block.T, listed, mass_row),
    )
    ghost = lax.ppermute(face, dom, down)
    own_mass = jnp.pad(mass, (0, OWN_PAD - OWN))
    *tables, own_scale, wide = call(
        table_kernel,
        [
            (PICK, EXT, BF16),
            (ROWS, PICK, BF16),
            (PICK, HALF),
            (OWN_PAD, HALF),
            (GAUSS, HALF),
        ],
        [
            pltpu.VMEM((16, HALF), F32),
            pltpu.VMEM((8, 2 * HALF), F32),
            pltpu.VMEM((ROWS, HALF), F32),
            pltpu.VMEM((HALF, HALF), F32),
            pltpu.VMEM((2 * HALF, HALF), F32),
            pltpu.VMEM((16, 2 * HALF), F32),
            pltpu.VMEM((8, GHOST_AT), F32),
        ],
        (spectrum, cell_scale, conn.T, listed, interp, potential.T, stiffness, mass_row),
        2,
    )
    tables = tuple(tables)

    scratch = [pltpu.VMEM((EXT, 2 * HALF), BF16), pltpu.VMEM((PICK, 2 * HALF), BF16)]
    own_shape, face_shape = (OWN_PAD, HALF), (FACE_PAD, HALF)
    *sums, ghost_scale = call(
        first_kernel,
        [own_shape, face_shape, face_shape, face_shape],
        scratch,
        (spectrum, own, ghost) + tables,
        1,
    )
    last = ()
    for step in range(DEG):
        own_sum, ghost_sum, bottom_sum = sums
        from_above = lax.ppermute(bottom_sum, dom, down)
        from_below = lax.ppermute(ghost_sum, dom, up)
        operands = (spectrum, own_sum, ghost_sum, from_below, from_above, spread, own_scale)
        operands = operands + (ghost_scale, own, ghost) + last
        last = (own, ghost)
        if step < DEG - 1:
            own, ghost, *sums = call(
                functools.partial(step_kernel, step),
                [own_shape, face_shape, own_shape, face_shape, face_shape],
                scratch,
                operands + tables,
                1,
            )
    (field,) = call(
        functools.partial(last_kernel, DEG - 1),
        [(FIELD, HALF)],
        [],
        operands + (occupancy.reshape(1, HALF),),
        1,
    )
    whole = lax.all_gather(field, "orb", axis=0)

    weighted = field[:OWN_PAD] * own_mass[:, None]
    term = jnp.concatenate(
        [dot6(whole[half, :OWN_PAD], weighted, ((0,), (0,))) for half in range(2)], axis=0
    )
    near = ("xl", "zl", "yl")
    size = lax.axis_size(near)
    term = term * (1.0 / (count * OWN))
    pieces = lax.all_to_all(term.reshape(size, ORBS // size, HALF), near, 0, 0)
    piece = jnp.sum(pieces, axis=0)
    for far in (("xh", "zm"), ("zh", "yh")):
        piece = jnp.sum(gather_all(piece, far), axis=0)
    gram = lax.all_gather(gather_all(piece, near).reshape(ORBS, HALF), "orb", axis=0)

    (density,) = call(
        density_kernel,
        [(GAUSS, CELLS)],
        [
            pltpu.VMEM((ORBS, ORBS), F32),
            pltpu.VMEM((HALF, HALF), F32),
            pltpu.VMEM((EXT, 4 * HALF), BF16),
            pltpu.VMEM((CELLS, GAUSS, ORBS), F32),
        ],
        (gram, whole, tables[0], wide),
    )
    return density


def solution(mesh):
    side = round(mesh.shape["dom"] ** (1.0 / 3.0))
    half = side // 2
    quarter = max(1, half // 2)
    shape = (half, 2, quarter, half // quarter, 2, half, 2, 2)
    torus = Mesh(mesh.devices.reshape(shape), DOM + ("orb",))
    dom = DOM
    in_specs = (
        P("orb", dom),
        P(None, dom),
        P(dom),
        P(dom),
        P(None, dom),
        P(dom),
        P(),
        P(),
        P("orb"),
        P(),
    )
    return jax.shard_map(
        per_device, mesh=torus, in_specs=in_specs, out_specs=P(None, dom), check_vma=False
    )
```

```python
import functools

import jax
import jax.numpy as jnp
from jax import lax
from jax.experimental import pallas as pl
from jax.experimental.pallas import tpu as pltpu
from jax.sharding import Mesh
from jax.sharding import PartitionSpec as P

ORBS = 256
HALF = 128
DEG = 3
NPC = 125
GAUSS = 216
FACE = 169
OWN = 676
CELLS = 9
OWN_PAD = 680
FACE_PAD = 176
GHOST_AT = 768
EXT = 1024
PICK = CELLS * 128
ROWS = 1040
OCC_AT = OWN_PAD + FACE_PAD
FIELD = 864
DOM = ("x", "zh", "zl", "y")
VMEM = 24 * 1024 * 1024
F32 = jnp.float32
BF16 = jnp.bfloat16


def split(value):
    high = value.astype(BF16)
    return high, (value - high.astype(F32)).astype(BF16)


def dot(a, b, dims=((1,), (0,))):
    return lax.dot_general(a, b, (dims, ((), ())), preferred_element_type=F32)


def dot3(a, b, dims=((1,), (0,))):
    a_high, a_low = split(a)
    b_high, b_low = split(b)
    return dot(a_high, b_high, dims) + (dot(a_high, b_low, dims) + dot(a_low, b_high, dims))


def dot6(a, b, dims=((1,), (0,))):
    return lax.dot_general(
        a, b, (dims, ((), ())), precision=lax.Precision.HIGHEST, preferred_element_type=F32
    )


def put_split(ref, rows, value):
    high, low = split(value)
    ref[rows, 0:HALF] = high
    ref[rows, HALF : 2 * HALF] = low


def joined(value):
    return value[:, 0:HALF] + value[:, HALF : 2 * HALF]


def apply_cells(own, ghost, pick_ref, place_ref, matrix_ref, ext_ref, cell_ref, outs):
    ext_ref[OWN_PAD:GHOST_AT] = jnp.zeros((GHOST_AT - OWN_PAD, 2 * HALF), BF16)
    ext_ref[GHOST_AT + FACE_PAD : EXT] = jnp.zeros((EXT - GHOST_AT - FACE_PAD, 2 * HALF), BF16)
    put_split(ext_ref, slice(0, OWN_PAD), own)
    put_split(ext_ref, slice(GHOST_AT, GHOST_AT + FACE_PAD), ghost)
    picked = joined(dot(pick_ref[...], ext_ref[...]))
    for cell in range(CELLS):
        rows = slice(cell * 128, cell * 128 + 128)
        high, low = split(picked[rows])
        matrix_high, matrix_low = split(matrix_ref[rows])
        term = joined(dot(matrix_high, jnp.concatenate([high, low], axis=1)))
        put_split(cell_ref, rows, term + dot(matrix_low, high))
    total = joined(dot(place_ref[...], cell_ref[...]))
    own_out, ghost_out, bottom_out = outs
    own_out[...] = total[0:OWN_PAD]
    ghost_out[...] = total[OWN_PAD : OWN_PAD + FACE_PAD]
    bottom_out[...] = total[OWN_PAD + FACE_PAD : OWN_PAD + 2 * FACE_PAD]


def column(row):
    return jnp.broadcast_to(row, (HALF, HALF)).T


def one_hot(left, right):
    return jnp.where(left == right, 1.0, 0.0).astype(BF16)


def fetch(sources, targets, done):
    copies = [
        pltpu.make_async_copy(source, target, done.at[i])
        for i, (source, target) in enumerate(zip(sources, targets, strict=True))
    ]
    for copy in copies:
        copy.start()
    for copy in copies:
        copy.wait()


def face_kernel(*refs):
    face, own, spread, listed, terms, select, ext, block, bottom, mass, done = refs[3:]
    fetch(refs[:3], (block, bottom, mass), done)
    own[0:OWN] = block[...]
    own[OWN:OWN_PAD] = jnp.zeros((OWN_PAD - OWN, HALF), F32)
    ext[OWN_PAD:GHOST_AT] = jnp.zeros((GHOST_AT - OWN_PAD, 2 * HALF), BF16)
    put_split(ext, slice(0, OWN_PAD), own[...])
    listed[...] = jnp.full(listed.shape, -2.0, F32)
    listed[0:1, 0:FACE] = bottom[...].astype(F32)
    lane = lax.broadcasted_iota(jnp.int32, (1, HALF), 1).astype(F32)
    for at in range(0, FACE_PAD, HALF):
        size = min(HALF, FACE_PAD - at)
        wanted = column(listed[0:1, at : at + HALF])[0:size]
        for start in range(0, GHOST_AT, HALF):
            select[at : at + size, start : start + HALF] = one_hot(wanted, lane + float(start))
    node = lax.broadcasted_iota(jnp.int32, (GHOST_AT, 2 * HALF), 0).astype(F32)
    spread[...] = one_hot(node, listed[0:1])
    terms[...] = jnp.zeros(terms.shape, F32)
    terms[0:1, 0:OWN] = mass[...]
    rest = terms[0:1]
    for term in range(3):
        part = rest.astype(BF16).astype(F32)
        terms[term : term + 1] = part
        rest = rest - part
    parts = dot(terms[...].astype(BF16), spread[...])
    masses = parts[0:1] + (parts[1:2] + parts[2:3])
    face[...] = joined(dot(select[...], ext[...]))
    face[FACE : FACE + 1] = masses[:, 0:HALF]
    face[FACE + 1 : FACE + 2] = masses[:, HALF:]


def halfwidth_of(spectrum):
    low = jnp.full((1, HALF), spectrum[0], F32)
    high = jnp.full((1, HALF), spectrum[1], F32)
    return (high - low) * 0.5, (high + low) * 0.5


def table_kernel(*refs):
    pick, place, matrix, own_scale, wide, scalars = refs[8:14]
    nodes, listed, targets, square, points, weight, masses = refs[14:21]
    scales, spectrum, conn, bottom, interp, potential, stiffness, mass, done = refs[21:]
    targets_of = (spectrum, scales, conn, bottom, interp, potential, stiffness, mass)
    fetch(refs[:8], targets_of, done)
    nodes[...] = jnp.full(nodes.shape, -1.0, F32)
    own_node = conn[...] < OWN
    named = jnp.where(own_node, conn[...], conn[...] + (GHOST_AT - OWN))
    nodes[0:CELLS, 0:NPC] = named.astype(F32)
    listed[...] = jnp.full(listed.shape, -2.0, F32)
    listed[0:1, 0:FACE] = bottom[...].astype(F32)
    lane = lax.broadcasted_iota(jnp.int32, (1, HALF), 1).astype(F32)
    targets[...] = jnp.full(targets.shape, -2.0, F32)
    row = lax.broadcasted_iota(jnp.int32, (OWN_PAD, HALF), 0).astype(F32)
    targets[0:OWN_PAD] = row
    targets[OWN_PAD:OCC_AT] = row[0:FACE_PAD] + float(GHOST_AT)
    for at in range(0, FACE_PAD, HALF):
        size = min(HALF, FACE_PAD - at)
        targets[OCC_AT + at : OCC_AT + at + size] = column(listed[0:1, at : at + HALF])[0:size]
    square[...] = jnp.zeros(square.shape, F32)
    square[0:NPC, 0:NPC] = stiffness[...]
    points[...] = jnp.zeros(points.shape, F32)
    points[0:GAUSS, 0:NPC] = interp[...]
    wide[...] = points[0:GAUSS]
    weight[...] = jnp.zeros(weight.shape, F32)
    weight[0:CELLS, 0:GAUSS] = potential[...]
    flipped = jnp.concatenate([points[0:HALF].T, points[HALF:].T], axis=1)
    high, low = split(points[...])
    both = jnp.concatenate([high, low], axis=1)
    for cell in range(CELLS):
        rows = slice(cell * HALF, cell * HALF + HALF)
        named = nodes[cell : cell + 1]
        wanted = column(named)
        for start in range(0, EXT, HALF):
            pick[rows, start : start + HALF] = one_hot(wanted, lane + float(start))
        place[:, rows] = one_hot(targets[...], named)
        left_high, left_low = split(flipped * weight[cell : cell + 1])
        product = joined(dot(left_high, both)) + dot(left_low, high)
        matrix[rows] = product + scales[cell] * square[...]
    masses[...] = jnp.ones(masses.shape, F32)
    masses[0:1, 0:OWN] = mass[...]
    halfwidth, centre = halfwidth_of(spectrum)
    scalars[...] = jnp.zeros(scalars.shape, F32)
    scalars[0:1] = halfwidth
    scalars[1:2] = centre / halfwidth
    for at in range(0, OWN_PAD, HALF):
        size = min(HALF, OWN_PAD - at)
        own_scale[at : at + size] = 1.0 / (column(masses[0:1, at : at + HALF])[0:size] * halfwidth)


def first_kernel(
    scalars, own, ghost, pick, place, matrix, own_out, ghost_out, bottom_out, scale_out, ext, cell
):
    outs = (own_out, ghost_out, bottom_out)
    apply_cells(own[...], ghost[...], pick, place, matrix, ext, cell, outs)
    halfwidth = scalars[0:1]
    node = lax.broadcasted_iota(jnp.int32, (FACE_PAD, HALF), 0)
    for at in range(0, FACE_PAD, HALF):
        size = min(HALF, FACE_PAD - at)
        mass_row = FACE + at // HALF
        mass = column(ghost[mass_row : mass_row + 1])[0:size]
        live = (mass > 0.0) & (node[at : at + size] < FACE)
        scale = 1.0 / (jnp.where(live, mass, 1.0) * halfwidth)
        scale_out[at : at + size] = jnp.where(live, scale, 0.0)


def next_values(step, refs):
    (scalars, own_sum, ghost_sum, from_below, from_above, spread, own_scale, ghost_scale) = refs[:8]
    factor = 1.0 if step == 0 else 2.0
    high, low = split(from_below[...])
    arriving = jnp.concatenate([high, low], axis=1)
    arriving = jnp.concatenate([arriving, jnp.zeros((2 * HALF - FACE_PAD, 2 * HALF), BF16)], axis=0)
    arrived = joined(dot(spread[...], arriving))
    own = refs[8][...]
    ghost = refs[9][...]
    shift = scalars[1:2]
    new_own = factor * (own_scale[...] * (own_sum[...] + arrived[0:OWN_PAD]) - shift * own)
    new_ghost = factor * (ghost_scale[...] * (ghost_sum[...] + from_above[...]) - shift * ghost)
    if step > 0:
        new_own = new_own - refs[10][...]
        new_ghost = new_ghost - refs[11][...]
    return new_own, new_ghost


def step_kernel(step, *refs):
    n = 10 if step == 0 else 12
    pick, place, matrix = refs[n : n + 3]
    new_own_out, new_ghost_out, own_out, ghost_out, bottom_out, ext, cell = refs[n + 3 :]
    own, ghost = next_values(step, refs)
    new_own_out[...] = own
    new_ghost_out[...] = ghost
    apply_cells(own, ghost, pick, place, matrix, ext, cell, (own_out, ghost_out, bottom_out))


def last_kernel(step, *refs):
    occ, out = refs[12:]
    own, ghost = next_values(step, refs)
    out[0:OWN_PAD] = own
    out[OWN_PAD:OCC_AT] = ghost
    out[OCC_AT:FIELD] = jnp.broadcast_to(occ[...], (FIELD - OCC_AT, HALF))


def reciprocal(value):
    guess = pl.reciprocal(value, approx=True)
    guess = guess * (2.0 - value * guess)
    return guess * (2.0 - value * guess)


def eliminate(block):
    groups = HALF // 8
    rows = [block[8 * i : 8 * i + 8] for i in range(groups)]
    lane = lax.broadcasted_iota(jnp.int32, (1, HALF), 1)
    sub = lax.broadcasted_iota(jnp.int32, (8, 1), 0)
    for k in range(0, HALF, 2):
        group, at = divmod(k, 8)
        left = [jnp.broadcast_to(rows[i][:, k : k + 1], (8, HALF)) for i in range(group, groups)]
        right = [
            jnp.broadcast_to(rows[i][:, k + 1 : k + 2], (8, HALF)) for i in range(group, groups)
        ]
        a = left[0][at : at + 1]
        b = left[0][at + 1 : at + 2]
        d = right[0][at + 1 : at + 2]
        scale = reciprocal(a * d - b * b)
        here, beside = lane == k, lane == k + 1
        upper = jnp.where(here, 1.0, jnp.where(beside, 0.0, rows[group][at : at + 1]))
        under = jnp.where(here, 0.0, jnp.where(beside, 1.0, rows[group][at + 1 : at + 2]))
        first = (d * upper - b * under) * scale
        second = (a * under - b * upper) * scale
        for i in range(group, groups):
            new = jnp.where(here | beside, 0.0, rows[i])
            new = new - left[i - group] * first - right[i - group] * second
            rows[i] = jnp.where(sub > at + 1, new, rows[i]) if i == group else new
    done = jnp.concatenate(rows, axis=0)
    i = lax.broadcasted_iota(jnp.int32, (HALF, HALF), 0)
    j = lax.broadcasted_iota(jnp.int32, (HALF, HALF), 1)
    odd = lax.broadcasted_iota(jnp.int32, (HALF, 1), 0) % 2 == 1
    diagonal = jnp.sum(jnp.where(i == j, done, 0.0), axis=1, keepdims=True)
    below = jnp.sum(jnp.where(i == j + 1, done, 0.0), axis=1, keepdims=True)
    lower = jnp.where(i // 2 > j // 2, done, jnp.where(i == j, 1.0, 0.0))
    ratio = jnp.where(odd, below / pltpu.roll(diagonal, 1, 0), 0.0)
    lower = lower - ratio * pltpu.roll(lower, 1, 0)
    return lower * lax.rsqrt(diagonal - ratio * below)


def density_kernel(gram, field, pick, interp, out, inverse, work, ext, quad):
    work[...] = gram[0, 0:HALF]
    inverse[0:HALF, HALF:] = jnp.zeros((HALF, HALF), F32)

    def body(part, carry):
        block = eliminate(work[...])

        @pl.when(part == 0)
        def _():
            inverse[0:HALF, 0:HALF] = block
            side = dot6(gram[0, HALF:], block, ((1,), (1,)))
            inverse[HALF:, 0:HALF] = dot6(side, block)
            work[...] = gram[1, HALF:] - dot6(side, side, ((1,), (1,)))

        @pl.when(part == 1)
        def _():
            inverse[HALF:, HALF:] = block
            inverse[HALF:, 0:HALF] = -dot6(block, inverse[HALF:, 0:HALF])

        return carry

    ext[OWN_PAD:GHOST_AT] = jnp.zeros((GHOST_AT - OWN_PAD, 4 * HALF), BF16)
    ext[GHOST_AT + FACE_PAD : EXT] = jnp.zeros((EXT - GHOST_AT - FACE_PAD, 4 * HALF), BF16)
    for half in range(2):
        lanes = slice(half * HALF, half * HALF + HALF)
        low_lanes = slice(ORBS + half * HALF, ORBS + half * HALF + HALF)
        for rows, at in (
            (slice(0, OWN_PAD), slice(0, OWN_PAD)),
            (slice(GHOST_AT, GHOST_AT + FACE_PAD), slice(OWN_PAD, OCC_AT)),
        ):
            high, low = split(field[half, at])
            ext[rows, lanes] = high
            ext[rows, low_lanes] = low
    picked = dot(pick[...], ext[...])
    values = picked[:, 0:ORBS] + picked[:, ORBS:]
    for cell in range(CELLS):
        quad[cell] = dot3(interp[...], values[cell * 128 : cell * 128 + 128])
    lax.fori_loop(0, 2, body, 0)
    occ = jnp.concatenate([field[0, OCC_AT : OCC_AT + 1], field[1, OCC_AT : OCC_AT + 1]], axis=1)
    weights = occ * (1.0 / ORBS)
    inv_high, inv_low = split(inverse[...])
    for cell in range(CELLS):
        high, low = split(quad[cell])
        dims = ((1,), (1,))
        value = dot(high, inv_high, dims) + (dot(high, inv_low, dims) + dot(low, inv_high, dims))
        out[:, cell : cell + 1] = jnp.sum(value * value * weights, axis=1, keepdims=True)


def call(kernel, shapes, scratch, operands, far=0):
    out = [jax.ShapeDtypeStruct(shape[:2], (shape + (F32,))[2]) for shape in shapes]
    in_vmem = pl.BlockSpec(memory_space=pltpu.VMEM)
    specs = [pl.BlockSpec(memory_space=pltpu.HBM)] * far + [in_vmem] * (len(operands) - far)
    operands = list(operands)
    for i in range(far):
        operands[i] = pltpu.with_memory_space_constraint(operands[i], pltpu.HBM)
    return pl.pallas_call(
        kernel,
        out_shape=out,
        in_specs=specs,
        out_specs=[in_vmem] * len(out),
        scratch_shapes=scratch,
        compiler_params=pltpu.CompilerParams(vmem_limit_bytes=VMEM),
    )(*operands)


def gather_all(value, axes):
    count = lax.axis_size(axes)
    return lax.all_to_all(jnp.broadcast_to(value[None], (count,) + value.shape), axes, 0, 0)


def per_device(
    block, conn, bottom, cell_scale, potential, mass, stiffness, interp, occupancy, spectrum
):
    dom = DOM
    count = lax.axis_size(dom)
    down = [(i + 1, i) for i in range(count - 1)]
    up = [(i, i + 1) for i in range(count - 1)]
    listed = bottom.reshape(1, FACE)
    mass_row = mass.reshape(1, OWN)
    face, own, spread = call(
        face_kernel,
        [(FACE_PAD, HALF), (OWN_PAD, HALF), (GHOST_AT, 2 * HALF, BF16)],
        [
            pltpu.VMEM((8, 2 * HALF), F32),
            pltpu.VMEM((8, GHOST_AT), F32),
            pltpu.VMEM((FACE_PAD, GHOST_AT), BF16),
            pltpu.VMEM((GHOST_AT, 2 * HALF), BF16),
            pltpu.VMEM((OWN, HALF), F32),
            pltpu.VMEM((1, FACE), jnp.int32),
            pltpu.VMEM((1, OWN), F32),
            pltpu.SemaphoreType.DMA((3,)),
        ],
        (block.T, listed, mass_row),
        3,
    )
    ghost = lax.ppermute(face, dom, down)
    own_mass = jnp.pad(mass, (0, OWN_PAD - OWN))
    *tables, own_scale, wide, scalars = call(
        table_kernel,
        [
            (PICK, EXT, BF16),
            (ROWS, PICK, BF16),
            (PICK, HALF),
            (OWN_PAD, HALF),
            (GAUSS, HALF),
            (8, HALF),
        ],
        [
            pltpu.VMEM((16, HALF), F32),
            pltpu.VMEM((8, 2 * HALF), F32),
            pltpu.VMEM((ROWS, HALF), F32),
            pltpu.VMEM((HALF, HALF), F32),
            pltpu.VMEM((2 * HALF, HALF), F32),
            pltpu.VMEM((16, 2 * HALF), F32),
            pltpu.VMEM((8, GHOST_AT), F32),
            pltpu.SMEM((CELLS,), F32),
            pltpu.SMEM((2,), F32),
            pltpu.VMEM((CELLS, NPC), jnp.int32),
            pltpu.VMEM((1, FACE), jnp.int32),
            pltpu.VMEM((GAUSS, NPC), F32),
            pltpu.VMEM((CELLS, GAUSS), F32),
            pltpu.VMEM((NPC, NPC), F32),
            pltpu.VMEM((1, OWN), F32),
            pltpu.SemaphoreType.DMA((8,)),
        ],
        (spectrum, cell_scale, conn.T, listed, interp, potential.T, stiffness, mass_row),
        8,
    )
    tables = tuple(tables)

    scratch = [pltpu.VMEM((EXT, 2 * HALF), BF16), pltpu.VMEM((PICK, 2 * HALF), BF16)]
    own_shape, face_shape = (OWN_PAD, HALF), (FACE_PAD, HALF)
    *sums, ghost_scale = call(
        first_kernel,
        [own_shape, face_shape, face_shape, face_shape],
        scratch,
        (scalars, own, ghost) + tables,
    )
    last = ()
    for step in range(DEG):
        own_sum, ghost_sum, bottom_sum = sums
        from_above = lax.ppermute(bottom_sum, dom, down)
        from_below = lax.ppermute(ghost_sum, dom, up)
        operands = (scalars, own_sum, ghost_sum, from_below, from_above, spread, own_scale)
        operands = operands + (ghost_scale, own, ghost) + last
        last = (own, ghost)
        if step < DEG - 1:
            own, ghost, *sums = call(
                functools.partial(step_kernel, step),
                [own_shape, face_shape, own_shape, face_shape, face_shape],
                scratch,
                operands + tables,
            )
    (field,) = call(
        functools.partial(last_kernel, DEG - 1),
        [(FIELD, HALF)],
        [],
        operands + (occupancy.reshape(1, HALF),),
    )
    whole = lax.all_gather(field, "orb", axis=0)

    weighted = field[:OWN_PAD] * own_mass[:, None]
    term = jnp.concatenate(
        [dot6(whole[half, :OWN_PAD], weighted, ((0,), (0,))) for half in range(2)], axis=0
    )
    near, far = ("zl", "y"), ("x", "zh")
    size = lax.axis_size(near)
    term = term * (1.0 / (count * OWN))
    pieces = lax.all_to_all(term.reshape(size, ORBS // size, HALF), near, 0, 0)
    piece = jnp.sum(gather_all(jnp.sum(pieces, axis=0), far), axis=0)
    gram = lax.all_gather(gather_all(piece, near).reshape(ORBS, HALF), "orb", axis=0)

    (density,) = call(
        density_kernel,
        [(GAUSS, CELLS)],
        [
            pltpu.VMEM((ORBS, ORBS), F32),
            pltpu.VMEM((HALF, HALF), F32),
            pltpu.VMEM((EXT, 4 * HALF), BF16),
            pltpu.VMEM((CELLS, GAUSS, ORBS), F32),
        ],
        (gram, whole, tables[0], wide),
    )
    return density


def solution(mesh):
    side = round(mesh.shape["dom"] ** (1.0 / 3.0))
    shape = (side, side // 2, 2, side, 2)
    torus = Mesh(mesh.devices.reshape(shape), DOM + ("orb",))
    dom = DOM
    in_specs = (
        P("orb", dom),
        P(None, dom),
        P(dom),
        P(dom),
        P(None, dom),
        P(dom),
        P(),
        P(),
        P("orb"),
        P(),
    )
    return jax.shard_map(
        per_device, mesh=torus, in_specs=in_specs, out_specs=P(None, dom), check_vma=False
    )
```

```python
import functools

import jax
import jax.numpy as jnp
from jax import lax
from jax.experimental import pallas as pl
from jax.experimental.pallas import tpu as pltpu
from jax.sharding import Mesh
from jax.sharding import PartitionSpec as P

ORBS = 256
HALF = 128
DEG = 3
NPC = 125
GAUSS = 216
FACE = 169
OWN = 676
CELLS = 9
OWN_PAD = 680
FACE_PAD = 176
GHOST_AT = 768
EXT = 1024
PICK = CELLS * 128
ROWS = 1040
OCC_AT = OWN_PAD + FACE_PAD
FIELD = 864
DOM = ("x", "zh", "zl", "y")
VMEM = 24 * 1024 * 1024
F32 = jnp.float32
BF16 = jnp.bfloat16


def split(value):
    high = value.astype(BF16)
    return high, (value - high.astype(F32)).astype(BF16)


def dot(a, b, dims=((1,), (0,))):
    return lax.dot_general(a, b, (dims, ((), ())), preferred_element_type=F32)


def dot3(a, b, dims=((1,), (0,))):
    a_high, a_low = split(a)
    b_high, b_low = split(b)
    return dot(a_high, b_high, dims) + (dot(a_high, b_low, dims) + dot(a_low, b_high, dims))


def dot6(a, b, dims=((1,), (0,))):
    return lax.dot_general(
        a, b, (dims, ((), ())), precision=lax.Precision.HIGHEST, preferred_element_type=F32
    )


def put_split(ref, rows, value):
    high, low = split(value)
    ref[rows, 0:HALF] = high
    ref[rows, HALF : 2 * HALF] = low


def joined(value):
    return value[:, 0:HALF] + value[:, HALF : 2 * HALF]


def apply_cells(own, ghost, pick_ref, place_ref, matrix_ref, ext_ref, cell_ref, outs):
    ext_ref[OWN_PAD:GHOST_AT] = jnp.zeros((GHOST_AT - OWN_PAD, 2 * HALF), BF16)
    ext_ref[GHOST_AT + FACE_PAD : EXT] = jnp.zeros((EXT - GHOST_AT - FACE_PAD, 2 * HALF), BF16)
    put_split(ext_ref, slice(0, OWN_PAD), own)
    put_split(ext_ref, slice(GHOST_AT, GHOST_AT + FACE_PAD), ghost)
    picked = joined(dot(pick_ref[...], ext_ref[...]))
    for cell in range(CELLS):
        rows = slice(cell * 128, cell * 128 + 128)
        high, low = split(picked[rows])
        matrix_high, matrix_low = split(matrix_ref[rows])
        term = joined(dot(matrix_high, jnp.concatenate([high, low], axis=1)))
        put_split(cell_ref, rows, term + dot(matrix_low, high))
    total = joined(dot(place_ref[...], cell_ref[...]))
    own_out, ghost_out, bottom_out = outs
    own_out[...] = total[0:OWN_PAD]
    ghost_out[...] = total[OWN_PAD : OWN_PAD + FACE_PAD]
    bottom_out[...] = total[OWN_PAD + FACE_PAD : OWN_PAD + 2 * FACE_PAD]


def column(row):
    return jnp.broadcast_to(row, (HALF, HALF)).T


def one_hot(left, right):
    return jnp.where(left == right, 1.0, 0.0).astype(BF16)


def fetch(sources, targets, done):
    copies = [
        pltpu.make_async_copy(source, target, done.at[i])
        for i, (source, target) in enumerate(zip(sources, targets, strict=True))
    ]
    for copy in copies:
        copy.start()
    for copy in copies:
        copy.wait()


def face_kernel(*refs):
    face, own, spread, listed, terms, select, ext, block, bottom, mass, done = refs[3:]
    fetch(refs[:3], (block, bottom, mass), done)
    own[0:OWN] = block[...]
    own[OWN:OWN_PAD] = jnp.zeros((OWN_PAD - OWN, HALF), F32)
    ext[OWN_PAD:GHOST_AT] = jnp.zeros((GHOST_AT - OWN_PAD, 2 * HALF), BF16)
    put_split(ext, slice(0, OWN_PAD), own[...])
    listed[...] = jnp.full(listed.shape, -2.0, F32)
    listed[0:1, 0:FACE] = bottom[...].astype(F32)
    lane = lax.broadcasted_iota(jnp.int32, (1, HALF), 1).astype(F32)
    for at in range(0, FACE_PAD, HALF):
        size = min(HALF, FACE_PAD - at)
        wanted = column(listed[0:1, at : at + HALF])[0:size]
        for start in range(0, GHOST_AT, HALF):
            select[at : at + size, start : start + HALF] = one_hot(wanted, lane + float(start))
    node = lax.broadcasted_iota(jnp.int32, (GHOST_AT, 2 * HALF), 0).astype(F32)
    spread[...] = one_hot(node, listed[0:1])
    terms[...] = jnp.zeros(terms.shape, F32)
    terms[0:1, 0:OWN] = mass[...].reshape(1, OWN)
    rest = terms[0:1]
    for term in range(3):
        part = rest.astype(BF16).astype(F32)
        terms[term : term + 1] = part
        rest = rest - part
    parts = dot(terms[...].astype(BF16), spread[...])
    masses = parts[0:1] + (parts[1:2] + parts[2:3])
    face[...] = joined(dot(select[...], ext[...]))
    face[FACE : FACE + 1] = masses[:, 0:HALF]
    face[FACE + 1 : FACE + 2] = masses[:, HALF:]


def halfwidth_of(spectrum):
    low = jnp.full((1, HALF), spectrum[0], F32)
    high = jnp.full((1, HALF), spectrum[1], F32)
    return (high - low) * 0.5, (high + low) * 0.5


def table_kernel(*refs):
    pick, place, matrix, own_scale, wide, scalars = refs[8:14]
    nodes, listed, targets, square, points, weight, masses = refs[14:21]
    scales, spectrum, conn, bottom, interp, potential, stiffness, mass, done = refs[21:]
    targets_of = (spectrum, scales, conn, bottom, interp, potential, stiffness, mass)
    fetch(refs[:8], targets_of, done)
    nodes[...] = jnp.full(nodes.shape, -1.0, F32)
    own_node = conn[...] < OWN
    named = jnp.where(own_node, conn[...], conn[...] + (GHOST_AT - OWN))
    nodes[0:CELLS, 0:NPC] = named.astype(F32)
    listed[...] = jnp.full(listed.shape, -2.0, F32)
    listed[0:1, 0:FACE] = bottom[...].astype(F32)
    lane = lax.broadcasted_iota(jnp.int32, (1, HALF), 1).astype(F32)
    targets[...] = jnp.full(targets.shape, -2.0, F32)
    row = lax.broadcasted_iota(jnp.int32, (OWN_PAD, HALF), 0).astype(F32)
    targets[0:OWN_PAD] = row
    targets[OWN_PAD:OCC_AT] = row[0:FACE_PAD] + float(GHOST_AT)
    for at in range(0, FACE_PAD, HALF):
        size = min(HALF, FACE_PAD - at)
        targets[OCC_AT + at : OCC_AT + at + size] = column(listed[0:1, at : at + HALF])[0:size]
    square[...] = jnp.zeros(square.shape, F32)
    square[0:NPC, 0:NPC] = stiffness[...]
    points[...] = jnp.zeros(points.shape, F32)
    points[0:GAUSS, 0:NPC] = interp[...]
    wide[...] = points[0:GAUSS]
    weight[...] = jnp.zeros(weight.shape, F32)
    weight[0:CELLS, 0:GAUSS] = potential[...]
    flipped = jnp.concatenate([points[0:HALF].T, points[HALF:].T], axis=1)
    high, low = split(points[...])
    both = jnp.concatenate([high, low], axis=1)
    for cell in range(CELLS):
        rows = slice(cell * HALF, cell * HALF + HALF)
        named = nodes[cell : cell + 1]
        wanted = column(named)
        for start in range(0, EXT, HALF):
            pick[rows, start : start + HALF] = one_hot(wanted, lane + float(start))
        place[:, rows] = one_hot(targets[...], named)
        left_high, left_low = split(flipped * weight[cell : cell + 1])
        product = joined(dot(left_high, both)) + dot(left_low, high)
        matrix[rows] = product + scales[cell] * square[...]
    masses[...] = jnp.ones(masses.shape, F32)
    masses[0:1, 0:OWN] = mass[...].reshape(1, OWN)
    halfwidth, centre = halfwidth_of(spectrum)
    scalars[...] = jnp.zeros(scalars.shape, F32)
    scalars[0:1] = halfwidth
    scalars[1:2] = centre / halfwidth
    for at in range(0, OWN_PAD, HALF):
        size = min(HALF, OWN_PAD - at)
        own_scale[at : at + size] = 1.0 / (column(masses[0:1, at : at + HALF])[0:size] * halfwidth)


def first_kernel(
    scalars, own, ghost, pick, place, matrix, own_out, ghost_out, bottom_out, scale_out, ext, cell
):
    outs = (own_out, ghost_out, bottom_out)
    apply_cells(own[...], ghost[...], pick, place, matrix, ext, cell, outs)
    halfwidth = scalars[0:1]
    node = lax.broadcasted_iota(jnp.int32, (FACE_PAD, HALF), 0)
    for at in range(0, FACE_PAD, HALF):
        size = min(HALF, FACE_PAD - at)
        mass_row = FACE + at // HALF
        mass = column(ghost[mass_row : mass_row + 1])[0:size]
        live = (mass > 0.0) & (node[at : at + size] < FACE)
        scale = 1.0 / (jnp.where(live, mass, 1.0) * halfwidth)
        scale_out[at : at + size] = jnp.where(live, scale, 0.0)


def next_values(step, refs):
    (scalars, own_sum, ghost_sum, from_below, from_above, spread, own_scale, ghost_scale) = refs[:8]
    factor = 1.0 if step == 0 else 2.0
    high, low = split(from_below[...])
    arriving = jnp.concatenate([high, low], axis=1)
    arriving = jnp.concatenate([arriving, jnp.zeros((2 * HALF - FACE_PAD, 2 * HALF), BF16)], axis=0)
    arrived = joined(dot(spread[...], arriving))
    own = refs[8][...]
    ghost = refs[9][...]
    shift = scalars[1:2]
    new_own = factor * (own_scale[...] * (own_sum[...] + arrived[0:OWN_PAD]) - shift * own)
    new_ghost = factor * (ghost_scale[...] * (ghost_sum[...] + from_above[...]) - shift * ghost)
    if step > 0:
        new_own = new_own - refs[10][...]
        new_ghost = new_ghost - refs[11][...]
    return new_own, new_ghost


def step_kernel(step, *refs):
    n = 10 if step == 0 else 12
    pick, place, matrix = refs[n : n + 3]
    new_own_out, new_ghost_out, own_out, ghost_out, bottom_out, ext, cell = refs[n + 3 :]
    own, ghost = next_values(step, refs)
    new_own_out[...] = own
    new_ghost_out[...] = ghost
    apply_cells(own, ghost, pick, place, matrix, ext, cell, (own_out, ghost_out, bottom_out))


def last_kernel(step, *refs):
    occ, out = refs[12:]
    own, ghost = next_values(step, refs)
    out[0:OWN_PAD] = own
    out[OWN_PAD:OCC_AT] = ghost
    out[OCC_AT:FIELD] = jnp.broadcast_to(occ[...], (FIELD - OCC_AT, HALF))


def reciprocal(value):
    guess = pl.reciprocal(value, approx=True)
    guess = guess * (2.0 - value * guess)
    return guess * (2.0 - value * guess)


def eliminate(block):
    groups = HALF // 8
    rows = [block[8 * i : 8 * i + 8] for i in range(groups)]
    lane = lax.broadcasted_iota(jnp.int32, (1, HALF), 1)
    sub = lax.broadcasted_iota(jnp.int32, (8, 1), 0)
    for k in range(0, HALF, 2):
        group, at = divmod(k, 8)
        left = [jnp.broadcast_to(rows[i][:, k : k + 1], (8, HALF)) for i in range(group, groups)]
        right = [
            jnp.broadcast_to(rows[i][:, k + 1 : k + 2], (8, HALF)) for i in range(group, groups)
        ]
        a = left[0][at : at + 1]
        b = left[0][at + 1 : at + 2]
        d = right[0][at + 1 : at + 2]
        scale = reciprocal(a * d - b * b)
        here, beside = lane == k, lane == k + 1
        upper = jnp.where(here, 1.0, jnp.where(beside, 0.0, rows[group][at : at + 1]))
        under = jnp.where(here, 0.0, jnp.where(beside, 1.0, rows[group][at + 1 : at + 2]))
        first = (d * upper - b * under) * scale
        second = (a * under - b * upper) * scale
        for i in range(group, groups):
            new = jnp.where(here | beside, 0.0, rows[i])
            new = new - left[i - group] * first - right[i - group] * second
            rows[i] = jnp.where(sub > at + 1, new, rows[i]) if i == group else new
    done = jnp.concatenate(rows, axis=0)
    i = lax.broadcasted_iota(jnp.int32, (HALF, HALF), 0)
    j = lax.broadcasted_iota(jnp.int32, (HALF, HALF), 1)
    odd = lax.broadcasted_iota(jnp.int32, (HALF, 1), 0) % 2 == 1
    diagonal = jnp.sum(jnp.where(i == j, done, 0.0), axis=1, keepdims=True)
    below = jnp.sum(jnp.where(i == j + 1, done, 0.0), axis=1, keepdims=True)
    lower = jnp.where(i // 2 > j // 2, done, jnp.where(i == j, 1.0, 0.0))
    ratio = jnp.where(odd, below / pltpu.roll(diagonal, 1, 0), 0.0)
    lower = lower - ratio * pltpu.roll(lower, 1, 0)
    return lower * lax.rsqrt(diagonal - ratio * below)


def density_kernel(gram, field, pick, interp, out, inverse, work, ext, quad):
    work[...] = gram[0, 0:HALF]
    inverse[0:HALF, HALF:] = jnp.zeros((HALF, HALF), F32)

    def body(part, carry):
        block = eliminate(work[...])

        @pl.when(part == 0)
        def _():
            inverse[0:HALF, 0:HALF] = block
            side = dot6(gram[0, HALF:], block, ((1,), (1,)))
            inverse[HALF:, 0:HALF] = dot6(side, block)
            work[...] = gram[1, HALF:] - dot6(side, side, ((1,), (1,)))

        @pl.when(part == 1)
        def _():
            inverse[HALF:, HALF:] = block
            inverse[HALF:, 0:HALF] = -dot6(block, inverse[HALF:, 0:HALF])

        return carry

    ext[OWN_PAD:GHOST_AT] = jnp.zeros((GHOST_AT - OWN_PAD, 4 * HALF), BF16)
    ext[GHOST_AT + FACE_PAD : EXT] = jnp.zeros((EXT - GHOST_AT - FACE_PAD, 4 * HALF), BF16)
    for half in range(2):
        lanes = slice(half * HALF, half * HALF + HALF)
        low_lanes = slice(ORBS + half * HALF, ORBS + half * HALF + HALF)
        for rows, at in (
            (slice(0, OWN_PAD), slice(0, OWN_PAD)),
            (slice(GHOST_AT, GHOST_AT + FACE_PAD), slice(OWN_PAD, OCC_AT)),
        ):
            high, low = split(field[half, at])
            ext[rows, lanes] = high
            ext[rows, low_lanes] = low
    picked = dot(pick[...], ext[...])
    values = picked[:, 0:ORBS] + picked[:, ORBS:]
    for cell in range(CELLS):
        quad[cell] = dot3(interp[...], values[cell * 128 : cell * 128 + 128])
    lax.fori_loop(0, 2, body, 0)
    occ = [column(field[half, OCC_AT : OCC_AT + 1]) for half in range(2)]
    weights = jnp.concatenate(occ, axis=0)[:, 0:1] * (1.0 / ORBS)
    inv_high, inv_low = split(inverse[...])
    for cell in range(CELLS):
        high, low = split(quad[cell])
        dims = ((1,), (1,))
        value = dot(inv_high, high, dims) + (dot(inv_low, high, dims) + dot(inv_high, low, dims))
        out[cell : cell + 1] = jnp.sum(value * value * weights, axis=0, keepdims=True)


def call(kernel, shapes, scratch, operands, far=0):
    out = [jax.ShapeDtypeStruct(shape[:2], (shape + (F32,))[2]) for shape in shapes]
    in_vmem = pl.BlockSpec(memory_space=pltpu.VMEM)
    specs = [pl.BlockSpec(memory_space=pltpu.HBM)] * far + [in_vmem] * (len(operands) - far)
    operands = list(operands)
    for i in range(far):
        operands[i] = pltpu.with_memory_space_constraint(operands[i], pltpu.HBM)
    return pl.pallas_call(
        kernel,
        out_shape=out,
        in_specs=specs,
        out_specs=[in_vmem] * len(out),
        scratch_shapes=scratch,
        compiler_params=pltpu.CompilerParams(vmem_limit_bytes=VMEM),
    )(*operands)


def gather_all(value, axes):
    count = lax.axis_size(axes)
    return lax.all_to_all(jnp.broadcast_to(value[None], (count,) + value.shape), axes, 0, 0)


def per_device(
    block, conn, bottom, cell_scale, potential, mass, stiffness, interp, occupancy, spectrum
):
    dom = DOM
    count = lax.axis_size(dom)
    down = [(i + 1, i) for i in range(count - 1)]
    up = [(i, i + 1) for i in range(count - 1)]
    listed = bottom.reshape(1, FACE)
    mass_row = mass
    face, own, spread = call(
        face_kernel,
        [(FACE_PAD, HALF), (OWN_PAD, HALF), (GHOST_AT, 2 * HALF, BF16)],
        [
            pltpu.VMEM((8, 2 * HALF), F32),
            pltpu.VMEM((8, GHOST_AT), F32),
            pltpu.VMEM((FACE_PAD, GHOST_AT), BF16),
            pltpu.VMEM((GHOST_AT, 2 * HALF), BF16),
            pltpu.VMEM((OWN, HALF), F32),
            pltpu.VMEM((1, FACE), jnp.int32),
            pltpu.VMEM((OWN,), F32),
            pltpu.SemaphoreType.DMA((3,)),
        ],
        (block.T, listed, mass_row),
        3,
    )
    ghost = lax.ppermute(face, dom, down)
    own_mass = jnp.pad(mass, (0, OWN_PAD - OWN))
    *tables, own_scale, wide, scalars = call(
        table_kernel,
        [
            (PICK, EXT, BF16),
            (ROWS, PICK, BF16),
            (PICK, HALF),
            (OWN_PAD, HALF),
            (GAUSS, HALF),
            (8, HALF),
        ],
        [
            pltpu.VMEM((16, HALF), F32),
            pltpu.VMEM((8, 2 * HALF), F32),
            pltpu.VMEM((ROWS, HALF), F32),
            pltpu.VMEM((HALF, HALF), F32),
            pltpu.VMEM((2 * HALF, HALF), F32),
            pltpu.VMEM((16, 2 * HALF), F32),
            pltpu.VMEM((8, GHOST_AT), F32),
            pltpu.SMEM((CELLS,), F32),
            pltpu.SMEM((2,), F32),
            pltpu.VMEM((CELLS, NPC), jnp.int32),
            pltpu.VMEM((1, FACE), jnp.int32),
            pltpu.VMEM((GAUSS, NPC), F32),
            pltpu.VMEM((CELLS, GAUSS), F32),
            pltpu.VMEM((NPC, NPC), F32),
            pltpu.VMEM((OWN,), F32),
            pltpu.SemaphoreType.DMA((8,)),
        ],
        (spectrum, cell_scale, conn.T, listed, interp, potential.T, stiffness, mass_row),
        8,
    )
    tables = tuple(tables)

    scratch = [pltpu.VMEM((EXT, 2 * HALF), BF16), pltpu.VMEM((PICK, 2 * HALF), BF16)]
    own_shape, face_shape = (OWN_PAD, HALF), (FACE_PAD, HALF)
    *sums, ghost_scale = call(
        first_kernel,
        [own_shape, face_shape, face_shape, face_shape],
        scratch,
        (scalars, own, ghost) + tables,
    )
    last = ()
    for step in range(DEG):
        own_sum, ghost_sum, bottom_sum = sums
        from_above = lax.ppermute(bottom_sum, dom, down)
        from_below = lax.ppermute(ghost_sum, dom, up)
        operands = (scalars, own_sum, ghost_sum, from_below, from_above, spread, own_scale)
        operands = operands + (ghost_scale, own, ghost) + last
        last = (own, ghost)
        if step < DEG - 1:
            own, ghost, *sums = call(
                functools.partial(step_kernel, step),
                [own_shape, face_shape, own_shape, face_shape, face_shape],
                scratch,
                operands + tables,
            )
    (field,) = call(
        functools.partial(last_kernel, DEG - 1),
        [(FIELD, HALF)],
        [],
        operands + (occupancy.reshape(1, HALF),),
    )
    whole = lax.all_gather(field, "orb", axis=0)

    weighted = field[:OWN_PAD] * own_mass[:, None]
    term = jnp.concatenate(
        [dot6(whole[half, :OWN_PAD], weighted, ((0,), (0,))) for half in range(2)], axis=0
    )
    near = ("zl", "y")
    size = lax.axis_size(near)
    term = term * (1.0 / (count * OWN))
    pieces = lax.all_to_all(term.reshape(size, ORBS // size, HALF), near, 0, 0)
    piece = jnp.sum(pieces, axis=0)
    for far in ("zh", "x"):
        piece = jnp.sum(gather_all(piece, far), axis=0)
    gram = lax.all_gather(gather_all(piece, near).reshape(ORBS, HALF), "orb", axis=0)

    (density,) = call(
        density_kernel,
        [(CELLS, GAUSS)],
        [
            pltpu.VMEM((ORBS, ORBS), F32),
            pltpu.VMEM((HALF, HALF), F32),
            pltpu.VMEM((EXT, 4 * HALF), BF16),
            pltpu.VMEM((CELLS, GAUSS, ORBS), F32),
        ],
        (gram, whole, tables[0], wide),
    )
    return density.T


def solution(mesh):
    side = round(mesh.shape["dom"] ** (1.0 / 3.0))
    shape = (side, side // 2, 2, side, 2)
    torus = Mesh(mesh.devices.reshape(shape), DOM + ("orb",))
    dom = DOM
    in_specs = (
        P("orb", dom),
        P(None, dom),
        P(dom),
        P(dom),
        P(None, dom),
        P(dom),
        P(),
        P(),
        P("orb"),
        P(),
    )
    return jax.shard_map(
        per_device, mesh=torus, in_specs=in_specs, out_specs=P(None, dom), check_vma=False
    )
```

```python
import functools

import jax
import jax.numpy as jnp
from jax import lax
from jax.experimental import pallas as pl
from jax.experimental.pallas import tpu as pltpu
from jax.sharding import Mesh
from jax.sharding import PartitionSpec as P

ORBS = 256
HALF = 128
DEG = 3
NPC = 125
GAUSS = 216
FACE = 169
OWN = 676
CELLS = 9
OWN_PAD = 680
FACE_PAD = 176
GHOST_AT = 768
EXT = 1024
PICK = CELLS * 128
ROWS = 1040
OCC_AT = OWN_PAD + FACE_PAD
FIELD = 864
DOM = ("x", "zh", "zl", "y")
VMEM = 24 * 1024 * 1024
F32 = jnp.float32
BF16 = jnp.bfloat16


def split(value):
    high = value.astype(BF16)
    return high, (value - high.astype(F32)).astype(BF16)


def dot(a, b, dims=((1,), (0,))):
    return lax.dot_general(a, b, (dims, ((), ())), preferred_element_type=F32)


def dot3(a, b, dims=((1,), (0,))):
    a_high, a_low = split(a)
    b_high, b_low = split(b)
    return dot(a_high, b_high, dims) + (dot(a_high, b_low, dims) + dot(a_low, b_high, dims))


def dot6(a, b, dims=((1,), (0,))):
    return lax.dot_general(
        a, b, (dims, ((), ())), precision=lax.Precision.HIGHEST, preferred_element_type=F32
    )


def put_split(ref, rows, value):
    high, low = split(value)
    ref[rows, 0:HALF] = high
    ref[rows, HALF : 2 * HALF] = low


def joined(value):
    return value[:, 0:HALF] + value[:, HALF : 2 * HALF]


def apply_cells(own, ghost, pick_ref, place_ref, matrix_ref, ext_ref, cell_ref, outs):
    ext_ref[OWN_PAD:GHOST_AT] = jnp.zeros((GHOST_AT - OWN_PAD, 2 * HALF), BF16)
    ext_ref[GHOST_AT + FACE_PAD : EXT] = jnp.zeros((EXT - GHOST_AT - FACE_PAD, 2 * HALF), BF16)
    put_split(ext_ref, slice(0, OWN_PAD), own)
    put_split(ext_ref, slice(GHOST_AT, GHOST_AT + FACE_PAD), ghost)
    picked = joined(dot(pick_ref[...], ext_ref[...]))
    for cell in range(CELLS):
        rows = slice(cell * 128, cell * 128 + 128)
        high, low = split(picked[rows])
        matrix_high, matrix_low = split(matrix_ref[rows])
        term = joined(dot(matrix_high, jnp.concatenate([high, low], axis=1)))
        put_split(cell_ref, rows, term + dot(matrix_low, high))
    total = joined(dot(place_ref[...], cell_ref[...]))
    own_out, ghost_out, bottom_out = outs
    own_out[...] = total[0:OWN_PAD]
    ghost_out[...] = total[OWN_PAD : OWN_PAD + FACE_PAD]
    bottom_out[...] = total[OWN_PAD + FACE_PAD : OWN_PAD + 2 * FACE_PAD]


def column(row):
    return jnp.broadcast_to(row, (HALF, HALF)).T


def one_hot(left, right):
    return jnp.where(left == right, 1.0, 0.0).astype(BF16)


def fetch(sources, targets, done):
    copies = [
        pltpu.make_async_copy(source, target, done.at[i])
        for i, (source, target) in enumerate(zip(sources, targets, strict=True))
    ]
    for copy in copies:
        copy.start()
    for copy in copies:
        copy.wait()


def face_kernel(*refs):
    face, own, spread, listed, terms, select, ext, block, bottom, mass, done = refs[3:]
    fetch(refs[:3], (block, bottom, mass), done)
    own[0:OWN] = block[...]
    own[OWN:OWN_PAD] = jnp.zeros((OWN_PAD - OWN, HALF), F32)
    ext[OWN_PAD:GHOST_AT] = jnp.zeros((GHOST_AT - OWN_PAD, 2 * HALF), BF16)
    put_split(ext, slice(0, OWN_PAD), own[...])
    listed[...] = jnp.full(listed.shape, -2.0, F32)
    listed[0:1, 0:FACE] = bottom[...].astype(F32)
    lane = lax.broadcasted_iota(jnp.int32, (1, HALF), 1).astype(F32)
    for at in range(0, FACE_PAD, HALF):
        size = min(HALF, FACE_PAD - at)
        wanted = column(listed[0:1, at : at + HALF])[0:size]
        for start in range(0, GHOST_AT, HALF):
            select[at : at + size, start : start + HALF] = one_hot(wanted, lane + float(start))
    node = lax.broadcasted_iota(jnp.int32, (GHOST_AT, 2 * HALF), 0).astype(F32)
    spread[...] = one_hot(node, listed[0:1])
    terms[...] = jnp.zeros(terms.shape, F32)
    terms[0:1, 0:OWN] = mass[...].reshape(1, OWN)
    rest = terms[0:1]
    for term in range(3):
        part = rest.astype(BF16).astype(F32)
        terms[term : term + 1] = part
        rest = rest - part
    parts = dot(terms[...].astype(BF16), spread[...])
    masses = parts[0:1] + (parts[1:2] + parts[2:3])
    face[...] = joined(dot(select[...], ext[...]))
    face[FACE : FACE + 1] = masses[:, 0:HALF]
    face[FACE + 1 : FACE + 2] = masses[:, HALF:]


def halfwidth_of(spectrum):
    low = jnp.full((1, HALF), spectrum[0], F32)
    high = jnp.full((1, HALF), spectrum[1], F32)
    return (high - low) * 0.5, (high + low) * 0.5


def table_kernel(*refs):
    pick, place, matrix, own_scale, wide, scalars = refs[8:14]
    nodes, listed, targets, square, points, weight, masses = refs[14:21]
    scales, spectrum, conn, bottom, interp, potential, stiffness, mass, done = refs[21:]
    targets_of = (spectrum, scales, conn, bottom, interp, potential, stiffness, mass)
    fetch(refs[:8], targets_of, done)
    nodes[...] = jnp.full(nodes.shape, -1.0, F32)
    own_node = conn[...] < OWN
    named = jnp.where(own_node, conn[...], conn[...] + (GHOST_AT - OWN))
    nodes[0:CELLS, 0:NPC] = named.astype(F32)
    listed[...] = jnp.full(listed.shape, -2.0, F32)
    listed[0:1, 0:FACE] = bottom[...].astype(F32)
    lane = lax.broadcasted_iota(jnp.int32, (1, HALF), 1).astype(F32)
    targets[...] = jnp.full(targets.shape, -2.0, F32)
    row = lax.broadcasted_iota(jnp.int32, (OWN_PAD, HALF), 0).astype(F32)
    targets[0:OWN_PAD] = row
    targets[OWN_PAD:OCC_AT] = row[0:FACE_PAD] + float(GHOST_AT)
    for at in range(0, FACE_PAD, HALF):
        size = min(HALF, FACE_PAD - at)
        targets[OCC_AT + at : OCC_AT + at + size] = column(listed[0:1, at : at + HALF])[0:size]
    square[...] = jnp.zeros(square.shape, F32)
    square[0:NPC, 0:NPC] = stiffness[...]
    points[...] = jnp.zeros(points.shape, F32)
    points[0:GAUSS, 0:NPC] = interp[...]
    wide[...] = points[0:GAUSS]
    weight[...] = jnp.zeros(weight.shape, F32)
    weight[0:CELLS, 0:GAUSS] = potential[...]
    flipped = jnp.concatenate([points[0:HALF].T, points[HALF:].T], axis=1)
    high, low = split(points[...])
    both = jnp.concatenate([high, low], axis=1)
    for cell in range(CELLS):
        rows = slice(cell * HALF, cell * HALF + HALF)
        named = nodes[cell : cell + 1]
        wanted = column(named)
        for start in range(0, EXT, HALF):
            pick[rows, start : start + HALF] = one_hot(wanted, lane + float(start))
        place[:, rows] = one_hot(targets[...], named)
        left_high, left_low = split(flipped * weight[cell : cell + 1])
        product = joined(dot(left_high, both)) + dot(left_low, high)
        matrix[rows] = product + scales[cell] * square[...]
    masses[...] = jnp.ones(masses.shape, F32)
    masses[0:1, 0:OWN] = mass[...].reshape(1, OWN)
    halfwidth, centre = halfwidth_of(spectrum)
    scalars[...] = jnp.zeros(scalars.shape, F32)
    scalars[0:1] = halfwidth
    scalars[1:2] = centre / halfwidth
    for at in range(0, OWN_PAD, HALF):
        size = min(HALF, OWN_PAD - at)
        own_scale[at : at + size] = 1.0 / (column(masses[0:1, at : at + HALF])[0:size] * halfwidth)


def first_kernel(
    scalars, own, ghost, pick, place, matrix, own_out, ghost_out, bottom_out, scale_out, ext, cell
):
    outs = (own_out, ghost_out, bottom_out)
    apply_cells(own[...], ghost[...], pick, place, matrix, ext, cell, outs)
    halfwidth = scalars[0:1]
    node = lax.broadcasted_iota(jnp.int32, (FACE_PAD, HALF), 0)
    for at in range(0, FACE_PAD, HALF):
        size = min(HALF, FACE_PAD - at)
        mass_row = FACE + at // HALF
        mass = column(ghost[mass_row : mass_row + 1])[0:size]
        live = (mass > 0.0) & (node[at : at + size] < FACE)
        scale = 1.0 / (jnp.where(live, mass, 1.0) * halfwidth)
        scale_out[at : at + size] = jnp.where(live, scale, 0.0)


def next_values(step, refs):
    (scalars, own_sum, ghost_sum, from_below, from_above, spread, own_scale, ghost_scale) = refs[:8]
    factor = 1.0 if step == 0 else 2.0
    high, low = split(from_below[...])
    arriving = jnp.concatenate([high, low], axis=1)
    arriving = jnp.concatenate([arriving, jnp.zeros((2 * HALF - FACE_PAD, 2 * HALF), BF16)], axis=0)
    arrived = joined(dot(spread[...], arriving))
    own = refs[8][...]
    ghost = refs[9][...]
    shift = scalars[1:2]
    new_own = factor * (own_scale[...] * (own_sum[...] + arrived[0:OWN_PAD]) - shift * own)
    new_ghost = factor * (ghost_scale[...] * (ghost_sum[...] + from_above[...]) - shift * ghost)
    if step > 0:
        new_own = new_own - refs[10][...]
        new_ghost = new_ghost - refs[11][...]
    return new_own, new_ghost


def step_kernel(step, *refs):
    n = 10 if step == 0 else 12
    pick, place, matrix = refs[n : n + 3]
    new_own_out, new_ghost_out, own_out, ghost_out, bottom_out, ext, cell = refs[n + 3 :]
    own, ghost = next_values(step, refs)
    new_own_out[...] = own
    new_ghost_out[...] = ghost
    apply_cells(own, ghost, pick, place, matrix, ext, cell, (own_out, ghost_out, bottom_out))


def last_kernel(step, *refs):
    occ, out = refs[12:]
    own, ghost = next_values(step, refs)
    out[0:OWN_PAD] = own
    out[OWN_PAD:OCC_AT] = ghost
    out[OCC_AT:FIELD] = jnp.broadcast_to(occ[...], (FIELD - OCC_AT, HALF))


def reciprocal(value):
    guess = pl.reciprocal(value, approx=True)
    return guess * (2.0 - value * guess)


def eliminate(block):
    groups = HALF // 8
    rows = [block[8 * i : 8 * i + 8] for i in range(groups)]
    lane = lax.broadcasted_iota(jnp.int32, (1, HALF), 1)
    sub = lax.broadcasted_iota(jnp.int32, (8, 1), 0)
    for k in range(0, HALF, 2):
        group, at = divmod(k, 8)
        left = [jnp.broadcast_to(rows[i][:, k : k + 1], (8, HALF)) for i in range(group, groups)]
        right = [
            jnp.broadcast_to(rows[i][:, k + 1 : k + 2], (8, HALF)) for i in range(group, groups)
        ]
        a = left[0][at : at + 1]
        b = left[0][at + 1 : at + 2]
        d = right[0][at + 1 : at + 2]
        scale = reciprocal(a * d - b * b)
        here, beside = lane == k, lane == k + 1
        upper = jnp.where(here, 1.0, jnp.where(beside, 0.0, rows[group][at : at + 1]))
        under = jnp.where(here, 0.0, jnp.where(beside, 1.0, rows[group][at + 1 : at + 2]))
        first = (d * upper - b * under) * scale
        second = (a * under - b * upper) * scale
        for i in range(group, groups):
            new = jnp.where(here | beside, 0.0, rows[i])
            new = new - left[i - group] * first - right[i - group] * second
            rows[i] = jnp.where(sub > at + 1, new, rows[i]) if i == group else new
    done = jnp.concatenate(rows, axis=0)
    i = lax.broadcasted_iota(jnp.int32, (HALF, HALF), 0)
    j = lax.broadcasted_iota(jnp.int32, (HALF, HALF), 1)
    odd = lax.broadcasted_iota(jnp.int32, (HALF, 1), 0) % 2 == 1
    diagonal = jnp.sum(jnp.where(i == j, done, 0.0), axis=1, keepdims=True)
    below = jnp.sum(jnp.where(i == j + 1, done, 0.0), axis=1, keepdims=True)
    lower = jnp.where(i // 2 > j // 2, done, jnp.where(i == j, 1.0, 0.0))
    ratio = jnp.where(odd, below / pltpu.roll(diagonal, 1, 0), 0.0)
    lower = lower - ratio * pltpu.roll(lower, 1, 0)
    return lower * lax.rsqrt(diagonal - ratio * below)


def density_kernel(gram, field, pick, interp, out, inverse, work, ext, quad):
    work[...] = gram[0, 0:HALF]
    inverse[0:HALF, HALF:] = jnp.zeros((HALF, HALF), F32)

    def body(part, carry):
        block = eliminate(work[...])

        @pl.when(part == 0)
        def _():
            inverse[0:HALF, 0:HALF] = block
            side = dot6(gram[0, HALF:], block, ((1,), (1,)))
            inverse[HALF:, 0:HALF] = dot6(side, block)
            work[...] = gram[1, HALF:] - dot6(side, side, ((1,), (1,)))

        @pl.when(part == 1)
        def _():
            inverse[HALF:, HALF:] = block
            inverse[HALF:, 0:HALF] = -dot6(block, inverse[HALF:, 0:HALF])

        return carry

    ext[OWN_PAD:GHOST_AT] = jnp.zeros((GHOST_AT - OWN_PAD, 4 * HALF), BF16)
    ext[GHOST_AT + FACE_PAD : EXT] = jnp.zeros((EXT - GHOST_AT - FACE_PAD, 4 * HALF), BF16)
    for half in range(2):
        lanes = slice(half * HALF, half * HALF + HALF)
        low_lanes = slice(ORBS + half * HALF, ORBS + half * HALF + HALF)
        for rows, at in (
            (slice(0, OWN_PAD), slice(0, OWN_PAD)),
            (slice(GHOST_AT, GHOST_AT + FACE_PAD), slice(OWN_PAD, OCC_AT)),
        ):
            high, low = split(field[half, at])
            ext[rows, lanes] = high
            ext[rows, low_lanes] = low
    picked = dot(pick[...], ext[...])
    values = picked[:, 0:ORBS] + picked[:, ORBS:]
    for cell in range(CELLS):
        quad[cell] = dot3(interp[...], values[cell * 128 : cell * 128 + 128])
    lax.fori_loop(0, 2, body, 0)
    occ = [column(field[half, OCC_AT : OCC_AT + 1]) for half in range(2)]
    weights = jnp.concatenate(occ, axis=0)[:, 0:1] * (1.0 / ORBS)
    inv_high, inv_low = split(inverse[...])
    for cell in range(CELLS):
        high, low = split(quad[cell])
        dims = ((1,), (1,))
        value = dot(inv_high, high, dims) + (dot(inv_low, high, dims) + dot(inv_high, low, dims))
        out[cell : cell + 1] = jnp.sum(value * value * weights, axis=0, keepdims=True)


def call(kernel, shapes, scratch, operands, far=0):
    out = [jax.ShapeDtypeStruct(shape[:2], (shape + (F32,))[2]) for shape in shapes]
    in_vmem = pl.BlockSpec(memory_space=pltpu.VMEM)
    specs = [pl.BlockSpec(memory_space=pltpu.HBM)] * far + [in_vmem] * (len(operands) - far)
    operands = list(operands)
    for i in range(far):
        operands[i] = pltpu.with_memory_space_constraint(operands[i], pltpu.HBM)
    return pl.pallas_call(
        kernel,
        out_shape=out,
        in_specs=specs,
        out_specs=[in_vmem] * len(out),
        scratch_shapes=scratch,
        compiler_params=pltpu.CompilerParams(vmem_limit_bytes=VMEM),
    )(*operands)


def gather_all(value, axes):
    count = lax.axis_size(axes)
    return lax.all_to_all(jnp.broadcast_to(value[None], (count,) + value.shape), axes, 0, 0)


def per_device(
    block, conn, bottom, cell_scale, potential, mass, stiffness, interp, occupancy, spectrum
):
    dom = DOM
    count = lax.axis_size(dom)
    down = [(i + 1, i) for i in range(count - 1)]
    up = [(i, i + 1) for i in range(count - 1)]
    listed = bottom.reshape(1, FACE)
    mass_row = mass
    face, own, spread = call(
        face_kernel,
        [(FACE_PAD, HALF), (OWN_PAD, HALF), (GHOST_AT, 2 * HALF, BF16)],
        [
            pltpu.VMEM((8, 2 * HALF), F32),
            pltpu.VMEM((8, GHOST_AT), F32),
            pltpu.VMEM((FACE_PAD, GHOST_AT), BF16),
            pltpu.VMEM((GHOST_AT, 2 * HALF), BF16),
            pltpu.VMEM((OWN, HALF), F32),
            pltpu.VMEM((1, FACE), jnp.int32),
            pltpu.VMEM((OWN,), F32),
            pltpu.SemaphoreType.DMA((3,)),
        ],
        (block.T, listed, mass_row),
        3,
    )
    ghost = lax.ppermute(face, dom, down)
    own_mass = jnp.pad(mass, (0, OWN_PAD - OWN))
    *tables, own_scale, wide, scalars = call(
        table_kernel,
        [
            (PICK, EXT, BF16),
            (ROWS, PICK, BF16),
            (PICK, HALF),
            (OWN_PAD, HALF),
            (GAUSS, HALF),
            (8, HALF),
        ],
        [
            pltpu.VMEM((16, HALF), F32),
            pltpu.VMEM((8, 2 * HALF), F32),
            pltpu.VMEM((ROWS, HALF), F32),
            pltpu.VMEM((HALF, HALF), F32),
            pltpu.VMEM((2 * HALF, HALF), F32),
            pltpu.VMEM((16, 2 * HALF), F32),
            pltpu.VMEM((8, GHOST_AT), F32),
            pltpu.SMEM((CELLS,), F32),
            pltpu.SMEM((2,), F32),
            pltpu.VMEM((CELLS, NPC), jnp.int32),
            pltpu.VMEM((1, FACE), jnp.int32),
            pltpu.VMEM((GAUSS, NPC), F32),
            pltpu.VMEM((CELLS, GAUSS), F32),
            pltpu.VMEM((NPC, NPC), F32),
            pltpu.VMEM((OWN,), F32),
            pltpu.SemaphoreType.DMA((8,)),
        ],
        (spectrum, cell_scale, conn.T, listed, interp, potential.T, stiffness, mass_row),
        8,
    )
    tables = tuple(tables)

    scratch = [pltpu.VMEM((EXT, 2 * HALF), BF16), pltpu.VMEM((PICK, 2 * HALF), BF16)]
    own_shape, face_shape = (OWN_PAD, HALF), (FACE_PAD, HALF)
    *sums, ghost_scale = call(
        first_kernel,
        [own_shape, face_shape, face_shape, face_shape],
        scratch,
        (scalars, own, ghost) + tables,
    )
    last = ()
    for step in range(DEG):
        own_sum, ghost_sum, bottom_sum = sums
        from_above = lax.ppermute(bottom_sum, dom, down)
        from_below = lax.ppermute(ghost_sum, dom, up)
        operands = (scalars, own_sum, ghost_sum, from_below, from_above, spread, own_scale)
        operands = operands + (ghost_scale, own, ghost) + last
        last = (own, ghost)
        if step < DEG - 1:
            own, ghost, *sums = call(
                functools.partial(step_kernel, step),
                [own_shape, face_shape, own_shape, face_shape, face_shape],
                scratch,
                operands + tables,
            )
    (field,) = call(
        functools.partial(last_kernel, DEG - 1),
        [(FIELD, HALF)],
        [],
        operands + (occupancy.reshape(1, HALF),),
    )
    whole = lax.all_gather(field, "orb", axis=0)

    weighted = field[:OWN_PAD] * own_mass[:, None]
    term = jnp.concatenate(
        [dot6(whole[half, :OWN_PAD], weighted, ((0,), (0,))) for half in range(2)], axis=0
    )
    near = ("zl", "y")
    size = lax.axis_size(near)
    term = term * (1.0 / (count * OWN))
    pieces = lax.all_to_all(term.reshape(size, ORBS // size, HALF), near, 0, 0)
    piece = jnp.sum(pieces, axis=0)
    for far in ("zh", "x"):
        piece = jnp.sum(gather_all(piece, far), axis=0)
    gram = lax.all_gather(gather_all(piece, near).reshape(ORBS, HALF), "orb", axis=0)

    (density,) = call(
        density_kernel,
        [(CELLS, GAUSS)],
        [
            pltpu.VMEM((ORBS, ORBS), F32),
            pltpu.VMEM((HALF, HALF), F32),
            pltpu.VMEM((EXT, 4 * HALF), BF16),
            pltpu.VMEM((CELLS, GAUSS, ORBS), F32),
        ],
        (gram, whole, tables[0], wide),
    )
    return density.T


def solution(mesh):
    side = round(mesh.shape["dom"] ** (1.0 / 3.0))
    shape = (side, side // 2, 2, side, 2)
    torus = Mesh(mesh.devices.reshape(shape), DOM + ("orb",))
    dom = DOM
    in_specs = (
        P("orb", dom),
        P(None, dom),
        P(dom),
        P(dom),
        P(None, dom),
        P(dom),
        P(),
        P(),
        P("orb"),
        P(),
    )
    return jax.shard_map(
        per_device, mesh=torus, in_specs=in_specs, out_specs=P(None, dom), check_vma=False
    )
```
